512 devices in a mesh: dom: 512 (over x, z, y, core).
Axes of the slice: x: 4, y: 8, z: 8, core: 2. Of those that a mesh axis runs over, the one named last changes fastest.
Arguments:
- blocks: bfloat16 [65536, 128, 128], P('dom'), may hold values from 2.4e-05 to 0.161
- col_index: int32 [512, 128], P('dom'), may hold values from 0 to 79, as said below
- row_offsets: int32 [512, 33], P('dom'), may hold values from 0 to 128, as said below
- send_index: int32 [512, 6, 8], P('dom'), may hold values from 0 to 31, as said below
- deg_scale: float32 [2097152], P('dom'), may hold values from 0.5 to 1
- seeds: float32 [16, 2097152], P(None, 'dom'), may hold values from 0.25 to 2
Outputs:
- spread: float32 [16, 2097152], P(None, 'dom')
The draws below stay inside these ranges and needn't reach their ends.
Inputs may be any that keep to these rules, and one draw needn't show every extreme that they name: In every partition the offsets start at 0 and rise by 1 to 4 per block row; slots from row_offsets[p, 32] on are unused; some partition uses all 128 slots. `col_index`: the first slot of block row r names the partition's own block r; entries below 32 name own blocks, the others received blocks. `send_index`: each list names 8 distinct blocks of the sending partition; its six lists together name every one of its blocks.
All inputs are finite; a program needn't handle non-finite values.
Results may differ from the reference program's by a relative error of at most 0.0003.
Values may be sent and summed in bfloat16 or wider, within the bound.
No kernel may reach another device: no remote copies, remote signals or barrier semaphores. Data moves between devices by JAX's collectives and lax.ppermute only.
A program may use at most 64 MiB of HBM per device.

```python
import math
import jax
import jax.numpy as jnp
from jax import lax

C = 16
BLK = 128
RB = 32
MAXR = 4
ITERS = 4
HB = 8
NNZ = 128
EXT = 80
DOMAINS = 512
ROWS = 2097152
NNZ_ALL = 65536


def row_layout(key):
    first_key, second_key = jax.random.split(jax.random.fold_in(key, 11))
    counts = jax.random.randint(first_key, (DOMAINS, RB), 1, MAXR + 1)
    fullest = jax.random.randint(second_key, (), 0, DOMAINS)
    counts = jnp.where((jnp.arange(DOMAINS) == fullest)[:, None], MAXR, counts)
    offsets = jnp.concatenate([jnp.zeros((DOMAINS, 1), jnp.int32), jnp.cumsum(counts, axis=1).astype(jnp.int32)], axis=1)
    return (offsets, fullest)


def draw_row_offsets(key, part):
    offsets, fullest = row_layout(key)
    return offsets.astype(jnp.int32)


def draw_col_index(key, part):
    offsets, fullest = row_layout(key)
    slots = jnp.arange(NNZ, dtype=jnp.int32)
    starts = offsets[:, :RB]
    is_first = (starts[:, :, None] == slots[None, None, :]).astype(jnp.int32)
    own_row = jnp.sum(is_first * jnp.arange(RB, dtype=jnp.int32)[None, :, None], axis=1)
    has_first = jnp.sum(is_first, axis=1) > 0
    others = jax.random.randint(jax.random.fold_in(key, 23), (DOMAINS, NNZ), 0, EXT)
    columns = jnp.where(has_first, own_row, others)
    last = (jnp.arange(DOMAINS) == fullest)[:, None] & (slots == NNZ - 1)[None, :]
    columns = jnp.where(last, EXT - 1, columns)
    return columns.astype(jnp.int32)


def draw_send_index(key, part):
    keys = jax.random.split(jax.random.fold_in(key, 7), DOMAINS)
    perms = jax.vmap(lambda single: jax.random.permutation(single, RB))(keys)
    position = (jnp.arange(6)[:, None] * HB + jnp.arange(HB)[None, :]) % RB
    return perms[:, position].astype(jnp.int32)


def draw_blocks(key, part):
    offsets, fullest = row_layout(key)
    slots = jnp.arange(NNZ, dtype=jnp.int32)
    row_of = jnp.sum((offsets[:, 1:, None] <= slots[None, None, :]).astype(jnp.int32), axis=1)
    row_of = jnp.minimum(row_of, RB - 1).astype(jnp.int32)
    factor_key = jax.random.fold_in(key, 31)
    entry_key = jax.random.fold_in(key, 37)
    share = 1.0 / 16.0

    def one_domain(items):
        index, rows = items
        row_draw = jax.random.uniform(jax.random.fold_in(factor_key, index), (RB, BLK), jnp.float32)
        row_factor = 0.25 * jnp.exp(row_draw * math.log(4.0))
        per_slot = row_factor[rows]
        level = jax.random.uniform(jax.random.fold_in(entry_key, index), (NNZ, BLK, BLK), jnp.float32)
        near = level < share
        upper = jnp.clip(level / share, 0.0, 1.0)
        lower = jnp.clip((level - share) / (1.0 - share), 0.0, 1.0)
        strong = 0.04 * jnp.exp(upper * math.log(4.0))
        faint = 0.0001 * jnp.exp(lower * math.log(10.0))
        value = jnp.where(near, strong, faint) * per_slot[:, :, None]
        return value.astype(jnp.bfloat16)
    mapped = lax.map(one_domain, (jnp.arange(DOMAINS, dtype=jnp.int32), row_of))
    return mapped.reshape(NNZ_ALL, BLK, BLK)


def draw_seeds(key, part):
    level = jax.random.uniform(jax.random.fold_in(key, 43), (C, ROWS), jnp.float32)
    values = 0.25 * jnp.exp(level * math.log(8.0))
    return values.astype(jnp.float32)


def steps_of(stream_key, shape, cuts, low, largest):
    level, own = 1.0, jax.random.fold_in(stream_key, 6)
    for axis_at, shards_of in cuts:
        heights = jnp.exp(jax.random.uniform(jax.random.fold_in(own, axis_at), (shards_of,), jnp.float32, low / len(cuts), largest / len(cuts)))
        level = level * jnp.repeat(heights, shape[axis_at] // shards_of).reshape([-1 if axis == axis_at else 1 for axis in range(len(shape))])
    return level


def setup_inputs(seed: int = 0) -> dict:
    key_of = jax.random.split(jax.random.key(seed), 7)
    blocks = draw_blocks(jax.random.fold_in(key_of[6], 71), 0)
    col_index = draw_col_index(jax.random.fold_in(key_of[6], 71), 0)
    row_offsets = draw_row_offsets(jax.random.fold_in(key_of[6], 71), 0)
    send_index = draw_send_index(jax.random.fold_in(key_of[6], 71), 0)
    deg_scale = jnp.clip(jnp.exp(math.log(1.0) - 0.6931472 * jax.random.uniform(key_of[4], (ROWS,), jnp.float32) ** steps_of(key_of[4], (ROWS,), ((0, 512),), -0.2, 0.2)), 0.5, 1.0)
    seeds = draw_seeds(jax.random.fold_in(key_of[6], 71), 0)
    return dict(blocks=blocks, col_index=col_index, row_offsets=row_offsets, send_index=send_index, deg_scale=deg_scale, seeds=seeds)


OFFSETS = (1, -1, 2, -2, 4, -4)
ALPHA = 0.8


def reference(blocks, col_index, row_offsets, send_index, deg_scale, seeds):
    count = DOMAINS
    weights = blocks.reshape(count, NNZ, BLK, BLK)
    scale = deg_scale.reshape(count, RB, 1, BLK)
    base = seeds.reshape(C, count, RB, BLK).transpose(1, 2, 0, 3)
    slots = jnp.arange(NNZ)
    row_of = jnp.sum((row_offsets[:, 1:, None] <= slots[None, None, :]).astype(jnp.int32), axis=1)
    owners = jnp.arange(count)
    field = base

    def one_part(items):
        extended, weight, columns, rows = items
        picked = extended[columns].astype(jnp.float32)
        prods = jnp.einsum('kcj,kij->kci', picked, weight.astype(jnp.float32), precision=lax.Precision.HIGHEST)
        onehot = (rows[None, :] == jnp.arange(RB)[:, None]).astype(jnp.float32)
        return jnp.einsum('rk,kci->rci', onehot, prods, precision=lax.Precision.HIGHEST)

    for step in range(ITERS):
        scaled = (field * scale).astype(jnp.bfloat16)
        pieces = [scaled]
        for j in range(6):
            source = (owners - OFFSETS[j]) % count
            pieces.append(scaled[source[:, None], send_index[source, j]])
        extended = jnp.concatenate(pieces, axis=1)
        summed = lax.map(one_part, (extended, weights, col_index, row_of))
        field = ALPHA * scale * summed + (1.0 - ALPHA) * base
    return field.transpose(2, 0, 1, 3).reshape(C, count * RB * BLK)
```

```python
import functools

import jax
import jax.numpy as jnp
from jax import lax
from jax.experimental import pallas as pl
from jax.experimental.pallas import tpu as pltpu
from jax.sharding import PartitionSpec as P

ITERS = 4
ALPHA = 0.8

SRC_NEAR, SRC_FAR, SRC_SIDE, SRC_SIB, SRC_ZERO = 32, 56, 72, 96, 128


def chip_groups(count):
    return [[2 * c, 2 * c + 1] for c in range(count // 2)]


def matching(count, step):
    chips = count // 2
    pairs = []
    for c in range(chips):
        k = (c // step) % 2
        for core, other in ((k, c + step), (1 - k, c - step)):
            pairs.append((2 * c + core, 2 * (other % chips) + core))
    return pairs


def tables(me, lists, columns):
    k = me & 1
    chip = me >> 1
    first = k == 0
    up1 = ((chip ^ k) & 1) == 0
    up2 = (((chip >> 1) ^ k) & 1) == 0
    sel = jnp.where
    seq = jnp.arange(lists.shape[1], dtype=jnp.int32)

    def own(j):
        pick = (jnp.arange(6, dtype=jnp.int32) == j)[:, None]
        return jnp.sum(sel(pick, lists, 0), axis=0)

    def sib(u):
        return 32 + 8 * u + seq

    near = sel(up1, 3, 2)
    third = sel(first & up1, 1, sel(first | up1, near, 0))
    give = jnp.concatenate([own(k), own(near), own(third), own(sel(up2, 5, 4))])
    send = jnp.concatenate(
        [
            sel(first & ~up1, own(1), sib(1)),
            sel(first, sel(up1, own(2), sib(1)), sel(up1, own(0), sib(2))),
            sel(first & up1, sib(2), sel(up1, own(2), own(3))),
            sib(3),
            own(sel(up2, 4, 5)),
        ]
    )
    near1, near2 = SRC_NEAR + 8, SRC_NEAR + 16
    side0, side1, side2 = SRC_SIDE, SRC_SIDE + 8, SRC_SIDE + 16
    base = [
        sel(first, sel(up1, side1, near2), SRC_SIB),
        sel(first, SRC_SIB, sel(up1, near1, side0)),
        sel(up1, side0, sel(first, near1, near2)),
        sel(up1, near2, sel(first, side0, side1)),
        sel(up2, side2, SRC_FAR + 8),
        sel(up2, SRC_FAR + 8, side2),
    ]
    unit = (columns - 32) >> 3
    at = columns
    for j in range(6):
        at = sel(unit == j, base[j] + ((columns - 32) & 7), at)
    return give.astype(jnp.int32), send.astype(jnp.int32), at.astype(jnp.int32), k.reshape(1)


def first_kernel(give, seeds, scale, x_out, give_out):
    nrb = x_out.shape[0]
    for r in range(nrb):
        field = seeds[:, r * 128 : (r + 1) * 128]
        x_out[r] = (field * scale[r : r + 1, :]).astype(jnp.bfloat16)
    for i in range(32):
        give_out[i] = x_out[give[i]]


def pack_kernel(core, send, x, chip, near, far, src):
    src[0:32] = x[...]
    src[32:64] = chip[1 - core[0]]
    for i in range(24):
        near[i] = src[send[i]]
    for i in range(16):
        far[i] = src[send[24 + i]]


def step_kernel(last, core, give, at, offsets, x, chip, near, far, side, seeds, scale, blocks, *rest):
    if last:
        out, src = rest
    else:
        x_out, give_out, src = rest
    other = 1 - core[0]
    src[0:32] = x[...]
    src[SRC_NEAR : SRC_NEAR + 24] = near[...]
    src[SRC_FAR : SRC_FAR + 16] = far[...]
    src[SRC_SIDE : SRC_SIDE + 24] = side[other]
    src[SRC_SIB : SRC_SIB + 8] = chip[other, 0:8]
    src[SRC_ZERO] = jnp.zeros((16, 128), jnp.bfloat16)

    def row(r):
        start, end = offsets[r], offsets[r + 1]
        lhs, rhs = [], []
        for s in range(4):
            slot = jnp.minimum(start + s, 127)
            lhs.append(src[jnp.where(start + s < end, at[slot], SRC_ZERO)])
            rhs.append(blocks[slot])
        total = None
        for h in range(2):
            part = lax.dot_general(
                jnp.concatenate(lhs[2 * h : 2 * h + 2], axis=1),
                jnp.concatenate(rhs[2 * h : 2 * h + 2], axis=1),
                (((1,), (1,)), ((), ())),
                preferred_element_type=jnp.float32,
            )
            total = part if total is None else total + part
        s = scale[pl.ds(r, 1), :]
        where = pl.ds(pl.multiple_of(r * 128, 128), 128)
        field = ALPHA * s * total + (1.0 - ALPHA) * seeds[:, where]
        if last:
            out[:, where] = field
        else:
            x_out[r] = (field * s).astype(jnp.bfloat16)

    def group(g, carry):
        for i in range(4):
            row(g * 4 + i)
        return carry

    lax.fori_loop(0, 8, group, 0)
    if not last:
        for i in range(32):
            give_out[i] = x_out[give[i]]


SMEM = pl.BlockSpec(memory_space=pltpu.SMEM)
VMEM = pl.BlockSpec(memory_space=pltpu.VMEM)


def bf16(*shape):
    return jax.ShapeDtypeStruct(shape, jnp.bfloat16)


def on_device(count, blocks, col_index, row_offsets, send_index, deg_scale, seeds):
    me = lax.axis_index("dom")
    nrb = deg_scale.shape[0] // 128
    give, send, at, core = tables(me, send_index[0], col_index[0])
    offsets = row_offsets[0]
    scale = deg_scale.reshape(nrb, 128)
    groups = chip_groups(count)
    near_pairs, far_pairs = matching(count, 1), matching(count, 2)
    params = pltpu.CompilerParams(vmem_limit_bytes=16 << 20)

    x, gift = pl.pallas_call(
        first_kernel,
        out_shape=(bf16(nrb, 16, 128), bf16(32, 16, 128)),
        in_specs=[SMEM, VMEM, VMEM],
        out_specs=(VMEM, VMEM),
        compiler_params=params,
        name="first",
    )(give, seeds, scale)
    for step in range(ITERS):
        chip = lax.all_gather(gift, "dom", axis=0, axis_index_groups=groups, tiled=False)
        near, far = pl.pallas_call(
            pack_kernel,
            out_shape=(bf16(24, 16, 128), bf16(16, 16, 128)),
            in_specs=[SMEM, SMEM, VMEM, VMEM],
            out_specs=(VMEM, VMEM),
            scratch_shapes=[pltpu.VMEM((64, 16, 128), jnp.bfloat16)],
            compiler_params=params,
            name="pack",
        )(core, send, x, chip)
        far = lax.ppermute(far, "dom", far_pairs)
        near = lax.ppermute(near, "dom", near_pairs)
        side = lax.all_gather(
            jnp.concatenate([near[:16], far[:8]]), "dom", axis=0, axis_index_groups=groups, tiled=False
        )
        last = step == ITERS - 1
        out_shape = jax.ShapeDtypeStruct(seeds.shape, jnp.float32) if last else (bf16(nrb, 16, 128), bf16(32, 16, 128))
        result = pl.pallas_call(
            functools.partial(step_kernel, last),
            out_shape=out_shape,
            in_specs=[SMEM] * 4 + [VMEM] * 8,
            out_specs=VMEM if last else (VMEM, VMEM),
            scratch_shapes=[pltpu.VMEM((SRC_ZERO + 1, 16, 128), jnp.bfloat16)],
            compiler_params=params,
            name="last" if last else "step",
        )(core, give, at, offsets, x, chip, near, far, side, seeds, scale, blocks)
        if not last:
            x, gift = result
    return result


def solution(mesh):
    in_specs = (
        P("dom", None, None),
        P("dom", None),
        P("dom", None),
        P("dom", None, None),
        P("dom"),
        P(None, "dom"),
    )
    out_specs = P(None, "dom")
    return jax.shard_map(
        functools.partial(on_device, mesh.size), mesh=mesh, in_specs=in_specs, out_specs=out_specs, check_vma=False
    )
```

```python
import functools

import jax
import jax.numpy as jnp
from jax import lax
from jax.experimental import pallas as pl
from jax.experimental.pallas import tpu as pltpu
from jax.sharding import PartitionSpec as P

ITERS = 4
ALPHA = 0.8
RB, C, BLK, HB = 32, 16, 128, 8


SMEM = pl.BlockSpec(memory_space=pltpu.SMEM)
VMEM = pl.BlockSpec(memory_space=pltpu.VMEM)
ANY = pl.BlockSpec(memory_space=pl.ANY)
HBM = pl.BlockSpec(memory_space=pltpu.HBM)


def bf16(*shape):
    return jax.ShapeDtypeStruct(shape, jnp.bfloat16)


def f32(*shape):
    return jax.ShapeDtypeStruct(shape, jnp.float32)


def role():
    me = lax.axis_index("dom")
    k = me & 1
    chip = me >> 1
    return k, ((chip ^ k) & 1) == 0, (((chip >> 1) ^ k) & 1) == 0


def units():
    k, up1, up2 = role()
    sel = jnp.where
    first = k == 0
    mine = [
        sel(first & ~up1, 1, -1),
        sel(up1, sel(first, 2, 0), -1),
        sel(first & up1, -1, sel(up1, 2, 3)),
        sel(up2, 4, 5),
    ]
    gift = [
        sel(first, sel(up1, 3, 2), sel(up1, -1, 2)),
        sel(first, sel(up1, 1, -1), sel(up1, 3, -1)),
        sel(first | up1, -1, 0),
        sel(up2, 5, 4),
        k,
    ]
    return mine, gift


def pack(lists, x, mine_out, gift_out):
    for out, which in zip((mine_out, gift_out), units()):
        for at, unit in enumerate(which):
            for h in range(HB):
                block = jnp.where(unit < 0, RB, lists[jnp.maximum(unit, 0), 0, h])
                out[at * HB + h] = x[block]


def first_kernel(lists_any, seeds_any, scale_any, x_out, mine_out, gift_out, base_out, scale_out, lists, seeds, x, sems):
    copies = [
        pltpu.make_async_copy(lists_any, lists, sems.at[0]),
        pltpu.make_async_copy(seeds_any, seeds, sems.at[1]),
        pltpu.make_async_copy(scale_any, scale_out, sems.at[2]),
    ]
    for copy in copies:
        copy.start()
    for copy in copies[::-1]:
        copy.wait()
    for r in range(RB):
        field = seeds[:, r * BLK : (r + 1) * BLK]
        base_out[r] = (1.0 - ALPHA) * field
        x[r] = (field * scale_out[r : r + 1, :]).astype(jnp.bfloat16)
    x[RB] = jnp.zeros((C, BLK), jnp.bfloat16)
    x_out[...] = x[0:RB]
    pack(lists, x, mine_out, gift_out)


def merge_kernel(mine, chip, near, far, direct):
    sib = chip.at[1 - role()[0]]
    near[...] = mine[0:24] + sib[0:24]
    far[0:8] = sib[24:32]
    far[8:16] = mine[24:32]
    direct[...] = sib[32:40]


def arrange_kernel(offsets, blocks, out):
    def row(r, carry):
        for s in range(4):
            slot = jnp.minimum(offsets[0, r] + s, BLK - 1)
            out[r, s * BLK : (s + 1) * BLK, :] = blocks[slot].T
        return carry

    lax.fori_loop(0, RB, row, 0)


def early_kernel(index, x, direct, blocks, acc, src):
    src[0:RB] = x[...]
    src[RB : RB + HB] = direct[...]
    src[RB + HB] = jnp.zeros((C, BLK), jnp.bfloat16)
    for r in range(RB):
        lhs = jnp.concatenate([src[index[r, s]] for s in range(4)], axis=1)
        acc[r] = jnp.dot(lhs, blocks[r], preferred_element_type=jnp.float32)


def late_kernel(last, index, lists_any, near, far, side, acc, base, scale, blocks, *rest):
    if last:
        out, src = rest
    else:
        x_out, mine_out, gift_out, src, x, lists, sem = rest
        copy = pltpu.make_async_copy(lists_any, lists, sem)
        copy.start()
    src[0:24] = near[...]
    src[24:40] = far[...]
    src[40:64] = side[1 - role()[0]]
    src[64] = jnp.zeros((C, BLK), jnp.bfloat16)
    at = [index[s : s + 1, :] for s in range(3)]
    for r in range(RB):
        lhs = jnp.concatenate([src[at[s][0, r]] for s in range(3)], axis=1)
        total = acc[r] + jnp.dot(lhs, blocks[r, BLK:, :], preferred_element_type=jnp.float32)
        s = scale[r : r + 1, :]
        field = ALPHA * s * total + base[r]
        if last:
            out[:, r * BLK : (r + 1) * BLK] = field
        else:
            x[r] = (field * s).astype(jnp.bfloat16)
    if not last:
        x[RB] = jnp.zeros((C, BLK), jnp.bfloat16)
        x_out[...] = x[0:RB]
        copy.wait()
        pack(lists, x, mine_out, gift_out)


def indices(columns, offsets):
    k, up1, up2 = role()
    sel = jnp.where
    first = k == 0
    base = [
        sel(first, sel(up1, 48, 16), -1),
        sel(first, -1, sel(up1, 8, 40)),
        sel(up1, 40, sel(first, 8, 16)),
        sel(up1, 16, sel(first, 40, 48)),
        sel(up2, 56, 32),
        sel(up2, 32, 56),
    ]
    inner = (columns - RB) & (HB - 1)
    own, got = columns, jnp.full_like(columns, 64)
    for j in range(6):
        here = (columns - RB) >> 3 == j
        own = sel(here, sel(base[j] < 0, RB + inner, RB + HB), own)
        got = sel(here & (base[j] >= 0), base[j] + inner, got)
    slots = jnp.arange(BLK, dtype=jnp.int32)
    start, end = offsets[:RB], offsets[1:]
    at = start[:, None] + jnp.arange(4, dtype=jnp.int32)[None, :]
    pick = (at[:, :, None] == slots) & (at < end[:, None])[:, :, None]
    own4 = jnp.sum(sel(pick, own - (RB + HB), 0), axis=2) + (RB + HB)
    got4 = jnp.sum(sel(pick, got - 64, 0), axis=2) + 64
    return own4.astype(jnp.int32), got4[:, 1:].T.astype(jnp.int32)


def on_device(count, blocks, col_index, row_offsets, send_index, deg_scale, seeds):
    groups = [[2 * c, 2 * c + 1] for c in range(count // 2)]

    def matching(step):
        chips = count // 2
        pairs = []
        for c in range(chips):
            k = (c // step) % 2
            for core, other in ((k, c + step), (1 - k, c - step)):
                pairs.append((2 * c + core, 2 * (other % chips) + core))
        return pairs

    def gather(value):
        return lax.all_gather(value, "dom", axis=0, axis_index_groups=groups, tiled=False)

    params = pltpu.CompilerParams(vmem_limit_bytes=16 << 20)
    call = functools.partial(pl.pallas_call, compiler_params=params)
    lists = jnp.transpose(send_index, (1, 0, 2))
    score = (C, BLK)

    x, mine, gift, base, scale = call(
        first_kernel,
        out_shape=(bf16(RB, *score), bf16(32, *score), bf16(40, *score), f32(RB, *score), f32(RB, BLK)),
        in_specs=[HBM] * 3,
        out_specs=(VMEM,) * 5,
        scratch_shapes=[
            pltpu.SMEM(lists.shape, jnp.int32),
            pltpu.VMEM(seeds.shape, jnp.float32),
            pltpu.VMEM((RB + 1, *score), jnp.bfloat16),
            pltpu.SemaphoreType.DMA((3,)),
        ],
        name="first",
    )(lists, seeds, deg_scale.reshape(RB, BLK))
    own_index, got_index = indices(col_index[0], row_offsets[0])
    arranged = None
    for step in range(ITERS):
        chip = gather(gift)
        near, far, direct = call(
            merge_kernel,
            out_shape=(bf16(24, *score), bf16(16, *score), bf16(HB, *score)),
            in_specs=[VMEM] * 2,
            out_specs=(VMEM,) * 3,
            name="merge",
        )(mine, chip)
        far = lax.ppermute(far, "dom", matching(2))
        near = lax.ppermute(near, "dom", matching(1))
        if arranged is None:
            arranged = call(
                arrange_kernel,
                out_shape=bf16(RB, 4 * BLK, BLK),
                in_specs=[SMEM, VMEM],
                out_specs=VMEM,
                cost_estimate=pl.CostEstimate(flops=0, bytes_accessed=16 << 20, transcendentals=0),
                name="arrange",
            )(row_offsets, blocks)
        acc = call(
            early_kernel,
            out_shape=f32(RB, *score),
            in_specs=[SMEM] + [VMEM] * 3,
            out_specs=VMEM,
            scratch_shapes=[pltpu.VMEM((RB + HB + 1, *score), jnp.bfloat16)],
            cost_estimate=pl.CostEstimate(flops=1 << 30, bytes_accessed=8 << 20, transcendentals=0),
            name="early",
        )(own_index, x, direct, arranged)
        side = gather(jnp.concatenate([near[:16], far[:8]]))
        last = step == ITERS - 1
        scratch = [pltpu.VMEM((65, *score), jnp.bfloat16)]
        if not last:
            scratch += [
                pltpu.VMEM((RB + 1, *score), jnp.bfloat16),
                pltpu.SMEM(lists.shape, jnp.int32),
                pltpu.SemaphoreType.DMA,
            ]
        result = call(
            functools.partial(late_kernel, last),
            out_shape=f32(*seeds.shape) if last else (bf16(RB, *score), bf16(32, *score), bf16(40, *score)),
            in_specs=[VMEM, ANY] + [VMEM] * 7,
            out_specs=VMEM if last else (VMEM,) * 3,
            scratch_shapes=scratch,
            name="last" if last else "late",
        )(got_index, lists, near, far, side, acc, base, scale, arranged)
        if not last:
            x, mine, gift = result
    return result


def solution(mesh):
    in_specs = (
        P("dom", None, None),
        P("dom", None),
        P("dom", None),
        P("dom", None, None),
        P("dom"),
        P(None, "dom"),
    )
    out_specs = P(None, "dom")
    return jax.shard_map(
        functools.partial(on_device, mesh.size), mesh=mesh, in_specs=in_specs, out_specs=out_specs, check_vma=False
    )
```

```python
import functools

import jax
import jax.numpy as jnp
from jax import lax
from jax.experimental import pallas as pl
from jax.experimental.pallas import tpu as pltpu
from jax.sharding import PartitionSpec as P

ITERS = 4
ALPHA = 0.8
RB, C, BLK, HB = 32, 16, 128, 8
ZERO = 72


SMEM = pl.BlockSpec(memory_space=pltpu.SMEM)
VMEM = pl.BlockSpec(memory_space=pltpu.VMEM)
ANY = pl.BlockSpec(memory_space=pl.ANY)
HBM = pl.BlockSpec(memory_space=pltpu.HBM)


def in_hbm(value):
    return pltpu.with_memory_space_constraint(value, pltpu.HBM)


def bf16(*shape):
    return jax.ShapeDtypeStruct(shape, jnp.bfloat16)


def f32(*shape):
    return jax.ShapeDtypeStruct(shape, jnp.float32)


def role():
    me = lax.axis_index("dom")
    k = me & 1
    chip = me >> 1
    return k, ((chip ^ k) & 1) == 1, (((chip >> 1) ^ k) & 1) == 0


def units():
    k, up1, up2 = role()
    sel = jnp.where
    first = k == 0
    mine = [
        sel(first & ~up1, 1, -1),
        sel(up1, sel(first, 2, 0), -1),
        sel(first & up1, -1, sel(up1, 2, 3)),
        sel(up2, 4, 5),
    ]
    gift = [
        sel(first, sel(up1, 3, 2), sel(up1, -1, 2)),
        sel(first, sel(up1, 1, -1), sel(up1, 3, -1)),
        sel(first | up1, -1, 0),
        sel(up2, 5, 4),
        k,
    ]
    return mine, gift


def pack(lists, x, mine_out, gift_out):
    for out, which in zip((mine_out, gift_out), units()):
        for at, unit in enumerate(which):
            for h in range(HB):
                block = jnp.where(unit < 0, RB, lists[jnp.maximum(unit, 0), 0, h])
                out[at * HB + h] = x[block]


def first_kernel(lists_any, seeds_any, scale_any, x_out, mine_out, gift_out, base_out, scale_out, lists, seeds, x, sems):
    copies = [
        pltpu.make_async_copy(lists_any, lists, sems.at[0]),
        pltpu.make_async_copy(seeds_any, seeds, sems.at[1]),
        pltpu.make_async_copy(scale_any, scale_out, sems.at[2]),
    ]
    for copy in copies:
        copy.start()
    for copy in copies[::-1]:
        copy.wait()
    for r in range(RB):
        field = seeds[:, r * BLK : (r + 1) * BLK]
        base_out[r] = (1.0 - ALPHA) * field
        x[r] = (field * scale_out[r : r + 1, :]).astype(jnp.bfloat16)
    x[RB] = jnp.zeros((C, BLK), jnp.bfloat16)
    x_out[...] = x[0:RB]
    pack(lists, x, mine_out, gift_out)


def merge_kernel(mine, chip, early, later, direct, both):
    k = role()[0]
    sib = chip.at[1 - k]
    both[0:24] = mine[0:24] + sib[0:24]
    both[24:32] = sib[24:32]
    both[32:40] = mine[24:32]
    both[40:48] = mine[24:32]
    early[...] = both[pl.ds(24 * k, 24)]
    later[...] = both[pl.ds(24 - 24 * k, 24)]
    direct[...] = sib[32:40]


def owe_kernel(early, later, out, both):
    k = role()[0]
    both[0:24] = early[...]
    both[24:48] = later[...]
    out[0:16] = both[pl.ds(24 * k, 16)]
    out[16:24] = both[pl.ds(24 - 24 * k, 8)]


def arrange_kernel(offsets_hbm, blocks_hbm, out, offsets, blocks, sems):
    first = pltpu.make_async_copy(offsets_hbm, offsets, sems.at[8])
    first.start()
    copies = []
    for g in range(8):
        part = pl.ds(16 * g, 16)
        copies.append(pltpu.make_async_copy(blocks_hbm.at[part], blocks.at[part], sems.at[g]))
        copies[-1].start()
    first.wait()
    for g in range(8):
        copies[g].wait()

        def row(r, carry):
            for s in range(4):
                slot = jnp.minimum(offsets[0, r] + s, 4 * r + 3)
                out[r, s * BLK : (s + 1) * BLK, :] = blocks[slot].T
            return carry

        lax.fori_loop(4 * g, 4 * g + 4, row, 0)


def early_kernel(index, x, direct, blocks, acc, src):
    src[0:RB] = x[...]
    src[RB : RB + HB] = direct[...]
    src[RB + HB] = jnp.zeros((C, BLK), jnp.bfloat16)
    for r in range(RB):
        lhs = jnp.concatenate([src[index[r, s]] for s in range(4)], axis=1)
        acc[r] = jnp.dot(lhs, blocks[r], preferred_element_type=jnp.float32)


def late_kernel(last, index, lists_any, early, later, side, acc, base, scale, blocks, *rest):
    if last:
        out, src = rest
    else:
        x_out, mine_out, gift_out, src, x, lists, sem = rest
        copy = pltpu.make_async_copy(lists_any, lists, sem)
        copy.start()
    src[0:24] = early[...]
    src[24:48] = later[...]
    src[48:72] = side[1 - role()[0]]
    src[ZERO] = jnp.zeros((C, BLK), jnp.bfloat16)
    at = [index[s : s + 1, :] for s in range(3)]
    for r in range(RB):
        lhs = jnp.concatenate([src[at[s][0, r]] for s in range(3)], axis=1)
        total = acc[r] + jnp.dot(lhs, blocks[r, BLK:, :], preferred_element_type=jnp.float32)
        s = scale[r : r + 1, :]
        field = ALPHA * s * total + base[r]
        if last:
            out[:, r * BLK : (r + 1) * BLK] = field
        else:
            x[r] = (field * s).astype(jnp.bfloat16)
    if not last:
        x[RB] = jnp.zeros((C, BLK), jnp.bfloat16)
        x_out[...] = x[0:RB]
        copy.wait()
        pack(lists, x, mine_out, gift_out)


def indices(columns, offsets):
    k, up1, up2 = role()
    sel = jnp.where
    first = k == 0
    near, far, side = 24 * k, 24 - 24 * k, 48
    base = [
        sel(first, sel(up1, side + 8, near + 16), -1),
        sel(first, -1, sel(up1, near + 8, side)),
        sel(up1, side, sel(first, near + 8, near + 16)),
        sel(up1, near + 16, sel(first, side, side + 8)),
        sel(up2, side + 16, far + 8),
        sel(up2, far + 8, side + 16),
    ]
    inner = (columns - RB) & (HB - 1)
    own, got = columns, jnp.full_like(columns, ZERO)
    for j in range(6):
        here = (columns - RB) >> 3 == j
        own = sel(here, sel(base[j] < 0, RB + inner, RB + HB), own)
        got = sel(here & (base[j] >= 0), base[j] + inner, got)
    slots = jnp.arange(BLK, dtype=jnp.int32)
    start, end = offsets[:RB], offsets[1:]
    at = start[:, None] + jnp.arange(4, dtype=jnp.int32)[None, :]
    pick = (at[:, :, None] == slots) & (at < end[:, None])[:, :, None]
    own4 = jnp.sum(sel(pick, own - (RB + HB), 0), axis=2) + (RB + HB)
    got4 = jnp.sum(sel(pick, got - ZERO, 0), axis=2) + ZERO
    return own4.astype(jnp.int32), got4[:, 1:].T.astype(jnp.int32)


def on_device(count, blocks, col_index, row_offsets, send_index, deg_scale, seeds):
    groups = [[2 * c, 2 * c + 1] for c in range(count // 2)]

    def pairs(crossing):
        chips = count // 2
        found = []
        for c in range(chips):
            if (c & 1) == crossing:
                found.append((2 * c + 1 - crossing, 2 * ((c + 1) % chips) + 1 - crossing))
            if (c >> 1 & 1) == crossing:
                found.append((2 * c + crossing, 2 * ((c + 2) % chips) + crossing))
        return found + [(b, a) for a, b in found]

    def gather(value):
        return lax.all_gather(value, "dom", axis=0, axis_index_groups=groups, tiled=False)

    params = pltpu.CompilerParams(vmem_limit_bytes=16 << 20)
    call = functools.partial(pl.pallas_call, compiler_params=params)
    lists = jnp.transpose(send_index, (1, 0, 2))
    score = (C, BLK)

    x, mine, gift, base, scale = call(
        first_kernel,
        out_shape=(bf16(RB, *score), bf16(32, *score), bf16(40, *score), f32(RB, *score), f32(RB, BLK)),
        in_specs=[HBM] * 3,
        out_specs=(VMEM,) * 5,
        scratch_shapes=[
            pltpu.SMEM(lists.shape, jnp.int32),
            pltpu.VMEM(seeds.shape, jnp.float32),
            pltpu.VMEM((RB + 1, *score), jnp.bfloat16),
            pltpu.SemaphoreType.DMA((3,)),
        ],
        name="first",
    )(in_hbm(lists), in_hbm(seeds), in_hbm(deg_scale.reshape(RB, BLK)))
    own_index, got_index = indices(col_index[0], row_offsets[0])
    arranged = None
    for step in range(ITERS):
        chip = gather(gift)
        early, later, direct = call(
            merge_kernel,
            out_shape=(bf16(24, *score), bf16(24, *score), bf16(HB, *score)),
            in_specs=[VMEM] * 2,
            out_specs=(VMEM,) * 3,
            scratch_shapes=[pltpu.VMEM((48, *score), jnp.bfloat16)],
            name="merge",
        )(mine, chip)
        early = lax.ppermute(early, "dom", pairs(1))
        later = lax.ppermute(later, "dom", pairs(0))
        if arranged is None:
            arranged = call(
                arrange_kernel,
                out_shape=bf16(RB, 4 * BLK, BLK),
                in_specs=[HBM, HBM],
                out_specs=VMEM,
                scratch_shapes=[
                    pltpu.SMEM(row_offsets.shape, jnp.int32),
                    pltpu.VMEM(blocks.shape, jnp.bfloat16),
                    pltpu.SemaphoreType.DMA((9,)),
                ],
                cost_estimate=pl.CostEstimate(flops=0, bytes_accessed=16 << 20, transcendentals=0),
                name="arrange",
            )(in_hbm(row_offsets), in_hbm(blocks))
        acc = call(
            early_kernel,
            out_shape=f32(RB, *score),
            in_specs=[SMEM] + [VMEM] * 3,
            out_specs=VMEM,
            scratch_shapes=[pltpu.VMEM((RB + HB + 1, *score), jnp.bfloat16)],
            cost_estimate=pl.CostEstimate(flops=1 << 30, bytes_accessed=8 << 20, transcendentals=0),
            name="early",
        )(own_index, x, direct, arranged)
        owed = call(
            owe_kernel,
            out_shape=bf16(24, *score),
            in_specs=[VMEM] * 2,
            out_specs=VMEM,
            scratch_shapes=[pltpu.VMEM((48, *score), jnp.bfloat16)],
            name="owe",
        )(early, later)
        side = gather(owed)
        last = step == ITERS - 1
        scratch = [pltpu.VMEM((ZERO + 1, *score), jnp.bfloat16)]
        if not last:
            scratch += [
                pltpu.VMEM((RB + 1, *score), jnp.bfloat16),
                pltpu.SMEM(lists.shape, jnp.int32),
                pltpu.SemaphoreType.DMA,
            ]
        result = call(
            functools.partial(late_kernel, last),
            out_shape=f32(*seeds.shape) if last else (bf16(RB, *score), bf16(32, *score), bf16(40, *score)),
            in_specs=[VMEM, ANY] + [VMEM] * 7,
            out_specs=VMEM if last else (VMEM,) * 3,
            scratch_shapes=scratch,
            name="last" if last else "late",
        )(got_index, lists, early, later, side, acc, base, scale, arranged)
        if not last:
            x, mine, gift = result
    return result


def solution(mesh):
    in_specs = (
        P("dom", None, None),
        P("dom", None),
        P("dom", None),
        P("dom", None, None),
        P("dom"),
        P(None, "dom"),
    )
    out_specs = P(None, "dom")
    return jax.shard_map(
        functools.partial(on_device, mesh.size), mesh=mesh, in_specs=in_specs, out_specs=out_specs, check_vma=False
    )
```

```python
import functools

import jax
import jax.numpy as jnp
from jax import lax
from jax.experimental import pallas as pl
from jax.experimental.pallas import tpu as pltpu
from jax.sharding import PartitionSpec as P

ITERS = 4
ALPHA = 0.8
RB, C, BLK, HB = 32, 16, 128, 8
SENT, PAIR, SIDE, DIRECT, ZERO = 32, 56, 80, 104, 112


SMEM = pl.BlockSpec(memory_space=pltpu.SMEM)
VMEM = pl.BlockSpec(memory_space=pltpu.VMEM)
ANY = pl.BlockSpec(memory_space=pl.ANY)
HBM = pl.BlockSpec(memory_space=pltpu.HBM)


def in_hbm(value):
    return pltpu.with_memory_space_constraint(value, pltpu.HBM)


def bf16(*shape):
    return jax.ShapeDtypeStruct(shape, jnp.bfloat16)


def f32(*shape):
    return jax.ShapeDtypeStruct(shape, jnp.float32)


def role():
    me = lax.axis_index("dom")
    k = me & 1
    chip = me >> 1
    return k, ((chip ^ k) & 1) == 1, (((chip >> 1) ^ k) & 1) == 0


def units():
    k, up1, up2 = role()
    sel = jnp.where
    first = k == 0
    mine = [
        sel(first & ~up1, 1, -1),
        sel(up1, sel(first, 2, 0), -1),
        sel(first & up1, -1, sel(up1, 2, 3)),
        sel(up2, 4, 5),
    ]
    gift = [
        sel(first, sel(up1, 3, 2), sel(up1, -1, 2)),
        sel(first, sel(up1, 1, -1), sel(up1, 3, -1)),
        sel(first | up1, -1, 0),
        sel(up2, 5, 4),
        k,
    ]
    return mine, gift


def pack(lists, x, mine_out, gift_out):
    for out, which in zip((mine_out, gift_out), units()):
        for at, unit in enumerate(which):
            for h in range(HB):
                block = jnp.where(unit < 0, RB, lists[jnp.maximum(unit, 0), 0, h])
                out[at * HB + h] = x[block]


def first_kernel(*refs):
    sources, (x_out, mine_out, gift_out, base_out, scale_out, columns, offsets, lists, seeds, x, sems) = refs[:5], refs[5:]
    copies = []
    for i, target in enumerate((seeds, scale_out, lists, columns, offsets)):
        copies.append(pltpu.make_async_copy(sources[i], target, sems.at[i]))
        copies[-1].start()
    for copy in copies:
        copy.wait()
    for r in range(RB):
        field = seeds[:, r * BLK : (r + 1) * BLK]
        base_out[r] = (1.0 - ALPHA) * field
        x[r] = (field * scale_out[r : r + 1, :]).astype(jnp.bfloat16)
    x[RB] = jnp.zeros((C, BLK), jnp.bfloat16)
    x_out[...] = x[0:RB]
    pack(lists, x, mine_out, gift_out)


def partner():
    me = lax.axis_index("dom")
    return 1 - jnp.where(me & 1 == 0, (me >> 2) & 1, (me >> 1) & 1)


def merge_kernel(mine, chip, cross, inner, both):
    k = role()[0]
    sib = chip.at[1 - k]
    both[0:24] = mine[0:24] + sib[0:24]
    both[24:32] = sib[24:32]
    both[32:40] = mine[24:32]
    both[40:48] = mine[24:32]
    cross[...] = both[pl.ds(24 * k, 24)]
    inner[...] = both[pl.ds(24 - 24 * k, 24)]


def owe_kernel(cross, pair, out, both):
    k = role()[0]
    both[0:24] = cross[...]
    both[24:48] = pair[partner()]
    out[0:16] = both[pl.ds(24 * k, 16)]
    out[16:24] = both[pl.ds(24 - 24 * k, 8)]


def arrange_kernel(offsets_any, blocks_hbm, out, offsets, blocks, sems):
    first = pltpu.make_async_copy(offsets_any, offsets, sems.at[8])
    first.start()
    copies = []
    for g in range(8):
        part = pl.ds(16 * g, 16)
        copies.append(pltpu.make_async_copy(blocks_hbm.at[part], blocks.at[part], sems.at[g]))
        copies[-1].start()
    first.wait()
    for g in range(8):
        copies[g].wait()
        for r in range(4 * g, 4 * g + 4):
            for s in range(4):
                slot = jnp.minimum(offsets[0, r] + s, 4 * r + 3)
                out[r, s * BLK : (s + 1) * BLK, :] = blocks[slot].T


def step_kernel(last, index, lists_any, x_in, chip, cross, pair, side, base, scale, blocks, *rest):
    if last:
        out, src = rest
    else:
        x_out, mine_out, gift_out, src, x, lists, sem = rest
        copy = pltpu.make_async_copy(lists_any, lists, sem)
        copy.start()
    other = 1 - role()[0]
    src[0:SENT] = x_in[...]
    src[SENT:PAIR] = cross[...]
    src[PAIR:SIDE] = pair[partner()]
    src[SIDE:DIRECT] = side[other]
    src[DIRECT:ZERO] = chip[other, 32:40]
    src[ZERO] = jnp.zeros((C, BLK), jnp.bfloat16)
    at = [index[s : s + 1, :] for s in range(4)]
    for r in range(RB):
        lhs = jnp.concatenate([src[at[s][0, r]] for s in range(4)], axis=1)
        total = jnp.dot(lhs, blocks[r], preferred_element_type=jnp.float32)
        s = scale[r : r + 1, :]
        field = ALPHA * s * total + base[r]
        if last:
            out[:, r * BLK : (r + 1) * BLK] = field
        else:
            x[r] = (field * s).astype(jnp.bfloat16)
    if not last:
        x[RB] = jnp.zeros((C, BLK), jnp.bfloat16)
        x_out[...] = x[0:RB]
        copy.wait()
        pack(lists, x, mine_out, gift_out)


def indices(columns, offsets):
    k, up1, up2 = role()
    sel = jnp.where
    first = k == 0
    near, far = sel(first, SENT, PAIR), sel(first, PAIR, SENT)
    base = [
        sel(first, sel(up1, SIDE + 8, near + 16), DIRECT),
        sel(first, DIRECT, sel(up1, near + 8, SIDE)),
        sel(up1, SIDE, sel(first, near + 8, near + 16)),
        sel(up1, near + 16, sel(first, SIDE, SIDE + 8)),
        sel(up2, SIDE + 16, far + 8),
        sel(up2, far + 8, SIDE + 16),
    ]
    where = columns
    for j in range(6):
        where = sel((columns - RB) >> 3 == j, base[j] + ((columns - RB) & (HB - 1)), where)
    slots = jnp.arange(BLK, dtype=jnp.int32)
    at = offsets[None, :RB] + jnp.arange(4, dtype=jnp.int32)[:, None]
    pick = (at[:, :, None] == slots) & (at < offsets[None, 1:])[:, :, None]
    return (jnp.sum(sel(pick, where - ZERO, 0), axis=2) + ZERO).astype(jnp.int32)


def on_device(count, blocks, col_index, row_offsets, send_index, deg_scale, seeds):
    chips = [[2 * c, 2 * c + 1] for c in range(count // 2)]

    def pairs(crossing):
        found = []
        for c in range(len(chips)):
            if (c & 1) == crossing:
                found.append((2 * c + 1 - crossing, 2 * ((c + 1) % len(chips)) + 1 - crossing))
            if (c >> 1 & 1) == crossing:
                found.append((2 * c + crossing, 2 * ((c + 2) % len(chips)) + crossing))
        return found

    def gather(value, groups):
        return lax.all_gather(value, "dom", axis=0, axis_index_groups=[list(g) for g in groups], tiled=False)

    params = pltpu.CompilerParams(vmem_limit_bytes=16 << 20)
    call = functools.partial(pl.pallas_call, compiler_params=params)
    lists = jnp.transpose(send_index, (1, 0, 2))
    score = (C, BLK)

    x, mine, gift, base, scale, columns, offsets = call(
        first_kernel,
        out_shape=(
            bf16(RB, *score),
            bf16(32, *score),
            bf16(40, *score),
            f32(RB, *score),
            f32(RB, BLK),
            jax.ShapeDtypeStruct(col_index.shape, jnp.int32),
            jax.ShapeDtypeStruct(row_offsets.shape, jnp.int32),
        ),
        in_specs=[HBM] * 5,
        out_specs=(VMEM,) * 7,
        scratch_shapes=[
            pltpu.SMEM(lists.shape, jnp.int32),
            pltpu.VMEM(seeds.shape, jnp.float32),
            pltpu.VMEM((RB + 1, *score), jnp.bfloat16),
            pltpu.SemaphoreType.DMA((5,)),
        ],
        name="first",
    )(*map(in_hbm, (seeds, deg_scale.reshape(RB, BLK), lists, col_index, row_offsets)))
    index = arranged = None
    for step in range(ITERS):
        chip = gather(gift, chips)
        cross, inner = call(
            merge_kernel,
            out_shape=(bf16(24, *score), bf16(24, *score)),
            in_specs=[VMEM] * 2,
            out_specs=(VMEM,) * 2,
            scratch_shapes=[pltpu.VMEM((48, *score), jnp.bfloat16)],
            name="merge",
        )(mine, chip)
        crossing = pairs(1)
        cross = lax.ppermute(cross, "dom", crossing + [(b, a) for a, b in crossing])
        pair = gather(inner, pairs(0))
        if arranged is None:
            pair, offsets, columns = lax.optimization_barrier((pair, offsets, columns))
            index = indices(columns[0], offsets[0])
            arranged = call(
                arrange_kernel,
                out_shape=bf16(RB, 4 * BLK, BLK),
                in_specs=[ANY, HBM],
                out_specs=VMEM,
                scratch_shapes=[
                    pltpu.SMEM(row_offsets.shape, jnp.int32),
                    pltpu.VMEM(blocks.shape, jnp.bfloat16),
                    pltpu.SemaphoreType.DMA((9,)),
                ],
                cost_estimate=pl.CostEstimate(flops=0, bytes_accessed=16 << 20, transcendentals=0),
                name="arrange",
            )(offsets, in_hbm(blocks))
        owed = call(
            owe_kernel,
            out_shape=bf16(24, *score),
            in_specs=[VMEM] * 2,
            out_specs=VMEM,
            scratch_shapes=[pltpu.VMEM((48, *score), jnp.bfloat16)],
            name="owe",
        )(cross, pair)
        side = gather(owed, chips)
        last = step == ITERS - 1
        scratch = [pltpu.VMEM((ZERO + 1, *score), jnp.bfloat16)]
        if not last:
            scratch += [
                pltpu.VMEM((RB + 1, *score), jnp.bfloat16),
                pltpu.SMEM(lists.shape, jnp.int32),
                pltpu.SemaphoreType.DMA,
            ]
        result = call(
            functools.partial(step_kernel, last),
            out_shape=f32(*seeds.shape) if last else (bf16(RB, *score), bf16(32, *score), bf16(40, *score)),
            in_specs=[VMEM, ANY] + [VMEM] * 8,
            out_specs=VMEM if last else (VMEM,) * 3,
            scratch_shapes=scratch,
            name="last" if last else "late",
        )(index, lists, x, chip, cross, pair, side, base, scale, arranged)
        if not last:
            x, mine, gift = result
    return result


def solution(mesh):
    in_specs = (
        P("dom", None, None),
        P("dom", None),
        P("dom", None),
        P("dom", None, None),
        P("dom"),
        P(None, "dom"),
    )
    out_specs = P(None, "dom")
    return jax.shard_map(
        functools.partial(on_device, mesh.size), mesh=mesh, in_specs=in_specs, out_specs=out_specs, check_vma=False
    )
```

```python
import functools

import jax
import jax.numpy as jnp
from jax import lax
from jax.experimental import pallas as pl
from jax.experimental.pallas import tpu as pltpu
from jax.sharding import PartitionSpec as P

ITERS = 4
ALPHA = 0.8
RB, C, BLK, HB = 32, 16, 128, 8
SENT, PAIR, SIDE, DIRECT, ZERO = 32, 56, 80, 104, 112


SMEM = pl.BlockSpec(memory_space=pltpu.SMEM)
VMEM = pl.BlockSpec(memory_space=pltpu.VMEM)
ANY = pl.BlockSpec(memory_space=pl.ANY)
HBM = pl.BlockSpec(memory_space=pltpu.HBM)


def in_hbm(value):
    return pltpu.with_memory_space_constraint(value, pltpu.HBM)


def bf16(*shape):
    return jax.ShapeDtypeStruct(shape, jnp.bfloat16)


def f32(*shape):
    return jax.ShapeDtypeStruct(shape, jnp.float32)


def role():
    me = lax.axis_index("dom")
    k = me & 1
    chip = me >> 1
    return k, ((chip ^ k) & 1) == 1, (((chip >> 1) ^ k) & 1) == 0


def units():
    k, up1, up2 = role()
    sel = jnp.where
    first = k == 0
    mine = [
        sel(first & ~up1, 1, -1),
        sel(up1, sel(first, 2, 0), -1),
        sel(first & up1, -1, sel(up1, 2, 3)),
        sel(up2, 4, 5),
    ]
    gift = [
        sel(first, sel(up1, 3, 2), sel(up1, -1, 2)),
        sel(first, sel(up1, 1, -1), sel(up1, 3, -1)),
        sel(first | up1, -1, 0),
        sel(up2, 5, 4),
        k,
    ]
    return mine, gift


def pack(lists, x, mine_out, gift_out):
    for out, which in zip((mine_out, gift_out), units()):
        for at, unit in enumerate(which):
            for h in range(HB):
                block = jnp.where(unit < 0, RB, lists[jnp.maximum(unit, 0), 0, h])
                out[at * HB + h] = x[block]


def first_kernel(*refs):
    sources, (x_out, mine_out, gift_out, base_out, scale_out, columns, offsets, lists, seeds, x, sems) = refs[:5], refs[5:]
    copies = []
    for i, target in enumerate((scale_out, lists, columns, offsets)):
        copies.append(pltpu.make_async_copy(sources[i + 1], target, sems.at[i]))
    for i in range(4):
        part = pl.ds(i * RB * BLK // 4, RB * BLK // 4)
        copies.append(pltpu.make_async_copy(sources[0].at[:, part], seeds.at[:, part], sems.at[i + 4]))
    for copy in copies:
        copy.start()
    for copy in copies[:4]:
        copy.wait()
    for r in range(RB):
        if r % 8 == 0:
            copies[4 + r // 8].wait()
        field = seeds[:, r * BLK : (r + 1) * BLK]
        base_out[r] = (1.0 - ALPHA) * field
        x[r] = (field * scale_out[r : r + 1, :]).astype(jnp.bfloat16)
    x[RB] = jnp.zeros((C, BLK), jnp.bfloat16)
    x_out[...] = x[0:RB]
    pack(lists, x, mine_out, gift_out)


def partner():
    me = lax.axis_index("dom")
    return 1 - jnp.where(me & 1 == 0, (me >> 2) & 1, (me >> 1) & 1)


def merge_kernel(mine, chip, cross, inner, both):
    k = role()[0]
    sib = chip.at[1 - k]
    both[0:24] = mine[0:24] + sib[0:24]
    both[24:32] = sib[24:32]
    both[32:40] = mine[24:32]
    both[40:48] = mine[24:32]
    cross[...] = both[pl.ds(24 * k, 24)]
    inner[...] = both[pl.ds(24 - 24 * k, 24)]


def owe_kernel(cross, pair, out, both):
    k = role()[0]
    both[0:24] = cross[...]
    both[24:48] = pair[partner()]
    out[0:16] = both[pl.ds(24 * k, 16)]
    out[16:24] = both[pl.ds(24 - 24 * k, 8)]


def arrange_kernel(offsets_any, blocks_hbm, out, offsets, blocks, sems):
    first = pltpu.make_async_copy(offsets_any, offsets, sems.at[8])
    first.start()
    copies = []
    for g in range(8):
        part = pl.ds(16 * g, 16)
        copies.append(pltpu.make_async_copy(blocks_hbm.at[part], blocks.at[part], sems.at[g]))
        copies[-1].start()
    first.wait()
    for g in range(8):
        copies[g].wait()
        for r in range(4 * g, 4 * g + 4):
            for s in range(4):
                slot = jnp.minimum(offsets[0, r] + s, 4 * r + 3)
                out[r, s * BLK : (s + 1) * BLK, :] = blocks[slot].T


def step_kernel(last, index, lists_any, x_in, chip, cross, pair, side, base, scale, blocks, *rest):
    if last:
        out_hbm, src, out, sems = rest
        parts = []
        for i in range(4):
            part = pl.ds(i * 8 * BLK, 8 * BLK)
            parts.append(pltpu.make_async_copy(out.at[:, part], out_hbm.at[:, part], sems.at[i]))
    else:
        x_out, mine_out, gift_out, src, x, lists, sem = rest
        copy = pltpu.make_async_copy(lists_any, lists, sem)
        copy.start()
    other = 1 - role()[0]
    src[0:SENT] = x_in[...]
    src[SENT:PAIR] = cross[...]
    src[PAIR:SIDE] = pair[partner()]
    src[SIDE:DIRECT] = side[other]
    src[DIRECT:ZERO] = chip[other, 32:40]
    src[ZERO] = jnp.zeros((C, BLK), jnp.bfloat16)
    at = [index[s : s + 1, :] for s in range(4)]

    @pl.when(other >= 0)
    def _():
        for r in range(RB):
            lhs = jnp.concatenate([src[at[s][0, r]] for s in range(4)], axis=1)
            total = jnp.dot(lhs, blocks[r], preferred_element_type=jnp.float32)
            s = scale[r : r + 1, :]
            field = ALPHA * s * total + base[r]
            if last:
                out[:, r * BLK : (r + 1) * BLK] = field
                if r % 8 == 7:
                    parts[r // 8].start()
            else:
                x[r] = (field * s).astype(jnp.bfloat16)

    if last:
        for part in parts:
            part.wait()
    else:
        x[RB] = jnp.zeros((C, BLK), jnp.bfloat16)
        x_out[...] = x[0:RB]
        copy.wait()
        pack(lists, x, mine_out, gift_out)


def indices(columns, offsets):
    k, up1, up2 = role()
    sel = jnp.where
    first = k == 0
    near, far = sel(first, SENT, PAIR), sel(first, PAIR, SENT)
    base = [
        sel(first, sel(up1, SIDE + 8, near + 16), DIRECT),
        sel(first, DIRECT, sel(up1, near + 8, SIDE)),
        sel(up1, SIDE, sel(first, near + 8, near + 16)),
        sel(up1, near + 16, sel(first, SIDE, SIDE + 8)),
        sel(up2, SIDE + 16, far + 8),
        sel(up2, far + 8, SIDE + 16),
    ]
    where = columns
    for j in range(6):
        where = sel((columns - RB) >> 3 == j, base[j] + ((columns - RB) & (HB - 1)), where)
    slots = jnp.arange(BLK, dtype=jnp.int32)
    at = offsets[None, :RB] + jnp.arange(4, dtype=jnp.int32)[:, None]
    pick = (at[:, :, None] == slots) & (at < offsets[None, 1:])[:, :, None]
    return (jnp.sum(sel(pick, where - ZERO, 0), axis=2) + ZERO).astype(jnp.int32)


def on_device(count, blocks, col_index, row_offsets, send_index, deg_scale, seeds):
    chips = [[2 * c, 2 * c + 1] for c in range(count // 2)]

    def pairs(crossing):
        found = []
        for c in range(len(chips)):
            if (c & 1) == crossing:
                found.append((2 * c + 1 - crossing, 2 * ((c + 1) % len(chips)) + 1 - crossing))
            if (c >> 1 & 1) == crossing:
                found.append((2 * c + crossing, 2 * ((c + 2) % len(chips)) + crossing))
        return found

    def gather(value, groups):
        return lax.all_gather(value, "dom", axis=0, axis_index_groups=[list(g) for g in groups], tiled=False)

    params = pltpu.CompilerParams(vmem_limit_bytes=16 << 20)
    call = functools.partial(pl.pallas_call, compiler_params=params)
    lists = jnp.transpose(send_index, (1, 0, 2))
    score = (C, BLK)

    x, mine, gift, base, scale, columns, offsets = call(
        first_kernel,
        out_shape=(
            bf16(RB, *score),
            bf16(32, *score),
            bf16(40, *score),
            f32(RB, *score),
            f32(RB, BLK),
            jax.ShapeDtypeStruct(col_index.shape, jnp.int32),
            jax.ShapeDtypeStruct(row_offsets.shape, jnp.int32),
        ),
        in_specs=[HBM] * 5,
        out_specs=(VMEM,) * 7,
        scratch_shapes=[
            pltpu.SMEM(lists.shape, jnp.int32),
            pltpu.VMEM(seeds.shape, jnp.float32),
            pltpu.VMEM((RB + 1, *score), jnp.bfloat16),
            pltpu.SemaphoreType.DMA((8,)),
        ],
        name="first",
    )(*map(in_hbm, (seeds, deg_scale.reshape(RB, BLK), lists, col_index, row_offsets)))
    index = arranged = None
    for step in range(ITERS):
        chip = gather(gift, chips)
        cross, inner = call(
            merge_kernel,
            out_shape=(bf16(24, *score), bf16(24, *score)),
            in_specs=[VMEM] * 2,
            out_specs=(VMEM,) * 2,
            scratch_shapes=[pltpu.VMEM((48, *score), jnp.bfloat16)],
            name="merge",
        )(mine, chip)
        crossing = pairs(1)
        cross = lax.ppermute(cross, "dom", crossing + [(b, a) for a, b in crossing])
        pair = gather(inner, pairs(0))
        if arranged is None:
            pair, offsets, columns = lax.optimization_barrier((pair, offsets, columns))
            index = indices(columns[0], offsets[0])
            arranged = call(
                arrange_kernel,
                out_shape=bf16(RB, 4 * BLK, BLK),
                in_specs=[ANY, HBM],
                out_specs=VMEM,
                scratch_shapes=[
                    pltpu.SMEM(row_offsets.shape, jnp.int32),
                    pltpu.VMEM(blocks.shape, jnp.bfloat16),
                    pltpu.SemaphoreType.DMA((9,)),
                ],
                cost_estimate=pl.CostEstimate(flops=0, bytes_accessed=16 << 20, transcendentals=0),
                name="arrange",
            )(offsets, in_hbm(blocks))
        owed = call(
            owe_kernel,
            out_shape=bf16(24, *score),
            in_specs=[VMEM] * 2,
            out_specs=VMEM,
            scratch_shapes=[pltpu.VMEM((48, *score), jnp.bfloat16)],
            name="owe",
        )(cross, pair)
        side = gather(owed, chips)
        last = step == ITERS - 1
        scratch = [pltpu.VMEM((ZERO + 1, *score), jnp.bfloat16)]
        if last:
            scratch += [pltpu.VMEM(seeds.shape, jnp.float32), pltpu.SemaphoreType.DMA((4,))]
        else:
            scratch += [
                pltpu.VMEM((RB + 1, *score), jnp.bfloat16),
                pltpu.SMEM(lists.shape, jnp.int32),
                pltpu.SemaphoreType.DMA,
            ]
        result = call(
            functools.partial(step_kernel, last),
            out_shape=f32(*seeds.shape) if last else (bf16(RB, *score), bf16(32, *score), bf16(40, *score)),
            in_specs=[VMEM, ANY] + [VMEM] * 8,
            out_specs=HBM if last else (VMEM,) * 3,
            scratch_shapes=scratch,
            name="last" if last else "late",
        )(index, lists, x, chip, cross, pair, side, base, scale, arranged)
        if not last:
            x, mine, gift = result
    return result


def solution(mesh):
    in_specs = (
        P("dom", None, None),
        P("dom", None),
        P("dom", None),
        P("dom", None, None),
        P("dom"),
        P(None, "dom"),
    )
    out_specs = P(None, "dom")
    return jax.shard_map(
        functools.partial(on_device, mesh.size), mesh=mesh, in_specs=in_specs, out_specs=out_specs, check_vma=False
    )
```

```python
import functools

import jax
import jax.numpy as jnp
from jax import lax
from jax.experimental import pallas as pl
from jax.experimental.pallas import tpu as pltpu
from jax.sharding import PartitionSpec as P

ITERS = 4
ALPHA = 0.8
RB, C, BLK, HB = 32, 16, 128, 8
SENT, PAIR, SIDE, DIRECT, ZERO = 32, 56, 80, 104, 112


SMEM = pl.BlockSpec(memory_space=pltpu.SMEM)
VMEM = pl.BlockSpec(memory_space=pltpu.VMEM)
ANY = pl.BlockSpec(memory_space=pl.ANY)
HBM = pl.BlockSpec(memory_space=pltpu.HBM)


def in_hbm(value):
    return pltpu.with_memory_space_constraint(value, pltpu.HBM)


def bf16(*shape):
    return jax.ShapeDtypeStruct(shape, jnp.bfloat16)


def f32(*shape):
    return jax.ShapeDtypeStruct(shape, jnp.float32)


def role():
    me = lax.axis_index("dom")
    k = me & 1
    chip = me >> 1
    return k, ((chip ^ k) & 1) == 1, (((chip >> 1) ^ k) & 1) == 0


def units():
    k, up1, up2 = role()
    sel = jnp.where
    first = k == 0
    mine = [
        sel(first & ~up1, 1, -1),
        sel(up1, sel(first, 2, 0), -1),
        sel(first & up1, -1, sel(up1, 2, 3)),
        sel(up2, 4, 5),
    ]
    gift = [
        sel(first, sel(up1, 3, 2), sel(up1, -1, 2)),
        sel(first, sel(up1, 1, -1), sel(up1, 3, -1)),
        sel(first | up1, -1, 0),
        sel(up2, 5, 4),
        k,
    ]
    return mine, gift


def pack(lists, x, mine_out, gift_out):
    for out, which in zip((mine_out, gift_out), units()):
        for at, unit in enumerate(which):
            for h in range(HB):
                block = jnp.where(unit < 0, RB, lists[jnp.maximum(unit, 0), 0, h])
                out[at * HB + h] = x[block]


def places(columns, offsets):
    k, up1, up2 = role()
    sel = jnp.where
    first = k == 0
    near, far = sel(first, SENT, PAIR), sel(first, PAIR, SENT)
    base = [
        sel(first, sel(up1, SIDE + 8, near + 16), DIRECT),
        sel(first, DIRECT, sel(up1, near + 8, SIDE)),
        sel(up1, SIDE, sel(first, near + 8, near + 16)),
        sel(up1, near + 16, sel(first, SIDE, SIDE + 8)),
        sel(up2, SIDE + 16, far + 8),
        sel(up2, far + 8, SIDE + 16),
    ]
    where = columns
    for j in range(6):
        where = sel((columns - RB) >> 3 == j, base[j] + ((columns - RB) & (HB - 1)), where)
    where = jnp.broadcast_to((where - ZERO).astype(jnp.float32), (8, BLK)).astype(jnp.bfloat16)
    start, end = offsets[:, :RB], offsets[:, 1:]
    slots = lax.broadcasted_iota(jnp.int32, (BLK, RB), 0)
    rows = []
    for s in range(4):
        pick = sel((slots == start + s) & (slots < end), 1.0, 0.0).astype(jnp.bfloat16)
        rows.append(jnp.dot(where, pick, preferred_element_type=jnp.float32)[0:1].astype(jnp.int32) + ZERO)
    return rows


def first_kernel(*refs):
    sources, (x_out, mine_out, gift_out, base_out, scale_out, index_out) = refs[:5], refs[5:11]
    lists, columns, offsets, seeds, x, sems = refs[11:]
    copies = []
    for i, target in enumerate((scale_out, lists, columns, offsets)):
        copies.append(pltpu.make_async_copy(sources[i + 1], target, sems.at[i]))
    for i in range(4):
        part = pl.ds(i * RB * BLK // 4, RB * BLK // 4)
        copies.append(pltpu.make_async_copy(sources[0].at[:, part], seeds.at[:, part], sems.at[i + 4]))
    for copy in copies:
        copy.start()
    for copy in copies[:4]:
        copy.wait()
    for s, row in enumerate(places(columns[...], offsets[...])):
        index_out[s : s + 1, :] = row
    for r in range(RB):
        if r % 8 == 0:
            copies[4 + r // 8].wait()
        field = seeds[:, r * BLK : (r + 1) * BLK]
        base_out[r] = (1.0 - ALPHA) * field
        x[r] = (field * scale_out[r : r + 1, :]).astype(jnp.bfloat16)
    x[RB] = jnp.zeros((C, BLK), jnp.bfloat16)
    x_out[...] = x[0:RB]
    pack(lists, x, mine_out, gift_out)


def partner():
    me = lax.axis_index("dom")
    return 1 - jnp.where(me & 1 == 0, (me >> 2) & 1, (me >> 1) & 1)


def merge_kernel(mine, chip, cross, inner, both):
    k = role()[0]
    sib = chip.at[1 - k]
    both[0:24] = mine[0:24] + sib[0:24]
    both[24:32] = sib[24:32]
    both[32:40] = mine[24:32]
    both[40:48] = mine[24:32]
    cross[...] = both[pl.ds(24 * k, 24)]
    inner[...] = both[pl.ds(24 - 24 * k, 24)]


def owe_kernel(cross, pair, out, both):
    k = role()[0]
    both[0:24] = cross[...]
    both[24:48] = pair[partner()]
    out[0:16] = both[pl.ds(24 * k, 16)]
    out[16:24] = both[pl.ds(24 - 24 * k, 8)]


def arrange_kernel(offsets_any, blocks_hbm, out, offsets, blocks, sems):
    first = pltpu.make_async_copy(offsets_any, offsets, sems.at[8])
    first.start()
    copies = []
    for g in range(8):
        part = pl.ds(16 * g, 16)
        copies.append(pltpu.make_async_copy(blocks_hbm.at[part], blocks.at[part], sems.at[g]))
        copies[-1].start()
    first.wait()
    for g in range(8):
        copies[g].wait()
        for r in range(4 * g, 4 * g + 4):
            for s in range(4):
                slot = jnp.minimum(offsets[0, r] + s, 4 * r + 3)
                out[r, s * BLK : (s + 1) * BLK, :] = blocks[slot].T


def step_kernel(last, index, lists_any, x_in, chip, cross, pair, side, base, scale, blocks, *rest):
    if last:
        out_hbm, src, out, sems = rest
        parts = []
        for i in range(4):
            part = pl.ds(i * 8 * BLK, 8 * BLK)
            parts.append(pltpu.make_async_copy(out.at[:, part], out_hbm.at[:, part], sems.at[i]))
    else:
        x_out, mine_out, gift_out, src, x, lists, sem = rest
        copy = pltpu.make_async_copy(lists_any, lists, sem)
        copy.start()
    other = 1 - role()[0]
    src[0:SENT] = x_in[...]
    src[SENT:PAIR] = cross[...]
    src[PAIR:SIDE] = pair[partner()]
    src[SIDE:DIRECT] = side[other]
    src[DIRECT:ZERO] = chip[other, 32:40]
    src[ZERO] = jnp.zeros((C, BLK), jnp.bfloat16)
    at = [index[s : s + 1, :] for s in range(4)]

    @pl.when(other >= 0)
    def _():
        for r in range(RB):
            lhs = jnp.concatenate([src[at[s][0, r]] for s in range(4)], axis=1)
            total = jnp.dot(lhs, blocks[r], preferred_element_type=jnp.float32)
            s = scale[r : r + 1, :]
            field = ALPHA * s * total + base[r]
            if last:
                out[:, r * BLK : (r + 1) * BLK] = field
                if r % 8 == 7:
                    parts[r // 8].start()
            else:
                x[r] = (field * s).astype(jnp.bfloat16)

    if last:
        for part in parts:
            part.wait()
    else:
        x[RB] = jnp.zeros((C, BLK), jnp.bfloat16)
        x_out[...] = x[0:RB]
        copy.wait()
        pack(lists, x, mine_out, gift_out)


def on_device(count, blocks, col_index, row_offsets, send_index, deg_scale, seeds):
    chips = [[2 * c, 2 * c + 1] for c in range(count // 2)]

    def pairs(crossing):
        found = []
        for c in range(len(chips)):
            if (c & 1) == crossing:
                found.append((2 * c + 1 - crossing, 2 * ((c + 1) % len(chips)) + 1 - crossing))
            if (c >> 1 & 1) == crossing:
                found.append((2 * c + crossing, 2 * ((c + 2) % len(chips)) + crossing))
        return found

    def gather(value, groups):
        return lax.all_gather(value, "dom", axis=0, axis_index_groups=[list(g) for g in groups], tiled=False)

    params = pltpu.CompilerParams(vmem_limit_bytes=16 << 20)
    call = functools.partial(pl.pallas_call, compiler_params=params)
    lists = jnp.transpose(send_index, (1, 0, 2))
    score = (C, BLK)

    x, mine, gift, base, scale, index = call(
        first_kernel,
        out_shape=(
            bf16(RB, *score),
            bf16(32, *score),
            bf16(40, *score),
            f32(RB, *score),
            f32(RB, BLK),
            jax.ShapeDtypeStruct((4, RB), jnp.int32),
        ),
        in_specs=[HBM] * 5,
        out_specs=(VMEM,) * 6,
        scratch_shapes=[
            pltpu.SMEM(lists.shape, jnp.int32),
            pltpu.VMEM(col_index.shape, jnp.int32),
            pltpu.VMEM(row_offsets.shape, jnp.int32),
            pltpu.VMEM(seeds.shape, jnp.float32),
            pltpu.VMEM((RB + 1, *score), jnp.bfloat16),
            pltpu.SemaphoreType.DMA((8,)),
        ],
        name="first",
    )(*map(in_hbm, (seeds, deg_scale.reshape(RB, BLK), lists, col_index, row_offsets)))
    arranged = None
    for step in range(ITERS):
        chip = gather(gift, chips)
        cross, inner = call(
            merge_kernel,
            out_shape=(bf16(24, *score), bf16(24, *score)),
            in_specs=[VMEM] * 2,
            out_specs=(VMEM,) * 2,
            scratch_shapes=[pltpu.VMEM((48, *score), jnp.bfloat16)],
            name="merge",
        )(mine, chip)
        crossing = pairs(1)
        cross = lax.ppermute(cross, "dom", crossing + [(b, a) for a, b in crossing])
        pair = gather(inner, pairs(0))
        if arranged is None:
            pair, row_offsets = lax.optimization_barrier((pair, row_offsets))
            arranged = call(
                arrange_kernel,
                out_shape=bf16(RB, 4 * BLK, BLK),
                in_specs=[HBM, HBM],
                out_specs=VMEM,
                scratch_shapes=[
                    pltpu.SMEM(row_offsets.shape, jnp.int32),
                    pltpu.VMEM(blocks.shape, jnp.bfloat16),
                    pltpu.SemaphoreType.DMA((9,)),
                ],
                cost_estimate=pl.CostEstimate(flops=0, bytes_accessed=16 << 20, transcendentals=0),
                name="arrange",
            )(in_hbm(row_offsets), in_hbm(blocks))
        owed = call(
            owe_kernel,
            out_shape=bf16(24, *score),
            in_specs=[VMEM] * 2,
            out_specs=VMEM,
            scratch_shapes=[pltpu.VMEM((48, *score), jnp.bfloat16)],
            name="owe",
        )(cross, pair)
        side = gather(owed, chips)
        last = step == ITERS - 1
        scratch = [pltpu.VMEM((ZERO + 1, *score), jnp.bfloat16)]
        if last:
            scratch += [pltpu.VMEM(seeds.shape, jnp.float32), pltpu.SemaphoreType.DMA((4,))]
        else:
            scratch += [
                pltpu.VMEM((RB + 1, *score), jnp.bfloat16),
                pltpu.SMEM(lists.shape, jnp.int32),
                pltpu.SemaphoreType.DMA,
            ]
        result = call(
            functools.partial(step_kernel, last),
            out_shape=f32(*seeds.shape) if last else (bf16(RB, *score), bf16(32, *score), bf16(40, *score)),
            in_specs=[VMEM, ANY] + [VMEM] * 8,
            out_specs=HBM if last else (VMEM,) * 3,
            scratch_shapes=scratch,
            name="last" if last else "late",
        )(index, lists, x, chip, cross, pair, side, base, scale, arranged)
        if not last:
            x, mine, gift = result
    return result


def solution(mesh):
    in_specs = (
        P("dom", None, None),
        P("dom", None),
        P("dom", None),
        P("dom", None, None),
        P("dom"),
        P(None, "dom"),
    )
    out_specs = P(None, "dom")
    return jax.shard_map(
        functools.partial(on_device, mesh.size), mesh=mesh, in_specs=in_specs, out_specs=out_specs, check_vma=False
    )
```

```python
import functools

import jax
import jax.numpy as jnp
from jax import lax
from jax.experimental import pallas as pl
from jax.experimental.pallas import tpu as pltpu
from jax.sharding import PartitionSpec as P

ITERS = 4
ALPHA = 0.8
RB, C, BLK, HB = 32, 16, 128, 8
SENT, PAIR, SIDE, DIRECT, ZERO = 32, 56, 80, 104, 112


SMEM = pl.BlockSpec(memory_space=pltpu.SMEM)
VMEM = pl.BlockSpec(memory_space=pltpu.VMEM)
ANY = pl.BlockSpec(memory_space=pl.ANY)
HBM = pl.BlockSpec(memory_space=pltpu.HBM)


def in_hbm(value):
    return pltpu.with_memory_space_constraint(value, pltpu.HBM)


def bf16(*shape):
    return jax.ShapeDtypeStruct(shape, jnp.bfloat16)


def f32(*shape):
    return jax.ShapeDtypeStruct(shape, jnp.float32)


def role():
    me = lax.axis_index("dom")
    k = me & 1
    chip = me >> 1
    return k, ((chip ^ k) & 1) == 1, (((chip >> 1) ^ k) & 1) == 0


def units():
    k, up1, up2 = role()
    sel = jnp.where
    first = k == 0
    mine = [
        sel(first & ~up1, 1, -1),
        sel(up1, sel(first, 2, 0), -1),
        sel(first & up1, -1, sel(up1, 2, 3)),
        sel(up2, 4, 5),
    ]
    gift = [
        sel(first, sel(up1, 3, 2), sel(up1, -1, 2)),
        sel(first, sel(up1, 1, -1), sel(up1, 3, -1)),
        sel(first | up1, -1, 0),
        sel(up2, 5, 4),
        k,
    ]
    return mine, gift


def pack(lists, x, mine_out, gift_out):
    for out, which in zip((mine_out, gift_out), units()):
        for at, unit in enumerate(which):
            for h in range(HB):
                block = jnp.where(unit < 0, RB, lists[jnp.maximum(unit, 0), 0, h])
                out[at * HB + h] = x[block]


def places(columns, offsets):
    k, up1, up2 = role()
    sel = jnp.where
    first = k == 0
    near, far = sel(first, SENT, PAIR), sel(first, PAIR, SENT)
    base = [
        sel(first, sel(up1, SIDE + 8, near + 16), DIRECT),
        sel(first, DIRECT, sel(up1, near + 8, SIDE)),
        sel(up1, SIDE, sel(first, near + 8, near + 16)),
        sel(up1, near + 16, sel(first, SIDE, SIDE + 8)),
        sel(up2, SIDE + 16, far + 8),
        sel(up2, far + 8, SIDE + 16),
    ]
    where = columns
    for j in range(6):
        where = sel((columns - RB) >> 3 == j, base[j] + ((columns - RB) & (HB - 1)), where)
    where = jnp.broadcast_to((where - ZERO).astype(jnp.float32), (8, BLK)).astype(jnp.bfloat16)
    start, end = offsets[:, :RB], offsets[:, 1:]
    slots = lax.broadcasted_iota(jnp.int32, (BLK, RB), 0)
    rows = []
    for s in range(4):
        pick = sel((slots == start + s) & (slots < end), 1.0, 0.0).astype(jnp.bfloat16)
        rows.append(jnp.dot(where, pick, preferred_element_type=jnp.float32)[0:1].astype(jnp.int32) + ZERO)
    return rows


def first_kernel(*refs):
    sources, (x_out, mine_out, gift_out, base_out, scale_out, index_out) = refs[:5], refs[5:11]
    lists, columns, offsets, seeds, x, sems = refs[11:]
    copies = []
    for i, target in enumerate((scale_out, lists, columns, offsets)):
        copies.append(pltpu.make_async_copy(sources[i + 1], target, sems.at[i]))
    for i in range(4):
        part = pl.ds(i * RB * BLK // 4, RB * BLK // 4)
        copies.append(pltpu.make_async_copy(sources[0].at[:, part], seeds.at[:, part], sems.at[i + 4]))
    for copy in copies:
        copy.start()
    for copy in copies[:4]:
        copy.wait()
    for s, row in enumerate(places(columns[...], offsets[...])):
        index_out[s : s + 1, :] = row
    for r in range(RB):
        if r % 8 == 0:
            copies[4 + r // 8].wait()
        field = seeds[:, r * BLK : (r + 1) * BLK]
        base_out[r] = (1.0 - ALPHA) * field
        x[r] = (field * scale_out[r : r + 1, :]).astype(jnp.bfloat16)
    x[RB] = jnp.zeros((C, BLK), jnp.bfloat16)
    x_out[...] = x[0:RB]
    pack(lists, x, mine_out, gift_out)


def partner(opening):
    me = lax.axis_index("dom")
    if opening:
        return 1 - jnp.where(me & 1 == 0, (me >> 2) & 1, (me >> 1) & 1)
    return ((me >> 1) ^ me) & 1


def merge_kernel(mine, chip, cross, inner, both):
    k = role()[0]
    sib = chip.at[1 - k]
    both[0:24] = mine[0:24] + sib[0:24]
    both[24:32] = sib[24:32]
    both[32:40] = mine[24:32]
    both[40:48] = mine[24:32]
    cross[...] = both[pl.ds(24 * k, 24)]
    inner[...] = both[pl.ds(24 - 24 * k, 24)]


def split_kernel(mine, chip, far, near):
    sib = chip.at[1 - role()[0]]
    near[...] = mine[0:24] + sib[0:24]
    far[0:8] = sib[24:32]
    far[8:16] = mine[24:32]


def owe_later_kernel(far, pair, out):
    out[0:16] = pair[partner(False), 0:16]
    out[16:24] = far[0:8]


def owe_kernel(cross, pair, out, both):
    k = role()[0]
    both[0:24] = cross[...]
    both[24:48] = pair[partner(True)]
    out[0:16] = both[pl.ds(24 * k, 16)]
    out[16:24] = both[pl.ds(24 - 24 * k, 8)]


def arrange_kernel(offsets_any, blocks_hbm, out, offsets, blocks, sems):
    first = pltpu.make_async_copy(offsets_any, offsets, sems.at[8])
    first.start()
    copies = []
    for g in range(8):
        part = pl.ds(16 * g, 16)
        copies.append(pltpu.make_async_copy(blocks_hbm.at[part], blocks.at[part], sems.at[g]))
        copies[-1].start()
    first.wait()
    for g in range(8):
        copies[g].wait()
        for r in range(4 * g, 4 * g + 4):
            for s in range(4):
                slot = jnp.minimum(offsets[0, r] + s, 4 * r + 3)
                out[r, s * BLK : (s + 1) * BLK, :] = blocks[slot].T


def step_kernel(opening, last, index, lists_any, x_in, chip, cross, pair, side, base, scale, blocks, *rest):
    if last:
        out_hbm, src, out, sems = rest
        parts = []
        for i in range(4):
            part = pl.ds(i * 8 * BLK, 8 * BLK)
            parts.append(pltpu.make_async_copy(out.at[:, part], out_hbm.at[:, part], sems.at[i]))
    else:
        x_out, mine_out, gift_out, src, x, lists, sem = rest
        copy = pltpu.make_async_copy(lists_any, lists, sem)
        copy.start()
    k = role()[0]
    other = 1 - k
    src[0:SENT] = x_in[...]
    if opening:
        src[SENT:PAIR] = cross[...]
        src[PAIR:SIDE] = pair[partner(True)]
    else:
        src[pl.ds(SENT + 24 * k, 24)] = pair[partner(False)]
        src[pl.ds(PAIR - 24 * k, 16)] = cross[...]
    src[SIDE:DIRECT] = side[other]
    src[DIRECT:ZERO] = chip[other, 32:40]
    src[ZERO] = jnp.zeros((C, BLK), jnp.bfloat16)
    at = [index[s : s + 1, :] for s in range(4)]

    @pl.when(other >= 0)
    def _():
        for r in range(RB):
            lhs = jnp.concatenate([src[at[s][0, r]] for s in range(4)], axis=1)
            total = jnp.dot(lhs, blocks[r], preferred_element_type=jnp.float32)
            s = scale[r : r + 1, :]
            field = ALPHA * s * total + base[r]
            if last:
                out[:, r * BLK : (r + 1) * BLK] = field
                if r % 8 == 7:
                    parts[r // 8].start()
            else:
                x[r] = (field * s).astype(jnp.bfloat16)

    if last:
        for part in parts:
            part.wait()
    else:
        x[RB] = jnp.zeros((C, BLK), jnp.bfloat16)
        x_out[...] = x[0:RB]
        copy.wait()
        pack(lists, x, mine_out, gift_out)


def on_device(count, blocks, col_index, row_offsets, send_index, deg_scale, seeds):
    chips = [[2 * c, 2 * c + 1] for c in range(count // 2)]

    def pairs(crossing):
        found = []
        for c in range(len(chips)):
            if (c & 1) == crossing:
                found.append((2 * c + 1 - crossing, 2 * ((c + 1) % len(chips)) + 1 - crossing))
            if (c >> 1 & 1) == crossing:
                found.append((2 * c + crossing, 2 * ((c + 2) % len(chips)) + crossing))
        return found

    def all_pairs(step):
        found = []
        for c in range(len(chips)):
            core = (c >> 1) & 1 if step == 2 else 1 - (c & 1)
            found.append((2 * c + core, 2 * ((c + step) % len(chips)) + core))
        return found

    def gather(value, groups):
        return lax.all_gather(value, "dom", axis=0, axis_index_groups=[list(g) for g in groups], tiled=False)

    params = pltpu.CompilerParams(vmem_limit_bytes=16 << 20)
    call = functools.partial(pl.pallas_call, compiler_params=params)
    lists = jnp.transpose(send_index, (1, 0, 2))
    score = (C, BLK)

    x, mine, gift, base, scale, index = call(
        first_kernel,
        out_shape=(
            bf16(RB, *score),
            bf16(32, *score),
            bf16(40, *score),
            f32(RB, *score),
            f32(RB, BLK),
            jax.ShapeDtypeStruct((4, RB), jnp.int32),
        ),
        in_specs=[HBM] * 5,
        out_specs=(VMEM,) * 6,
        scratch_shapes=[
            pltpu.SMEM(lists.shape, jnp.int32),
            pltpu.VMEM(col_index.shape, jnp.int32),
            pltpu.VMEM(row_offsets.shape, jnp.int32),
            pltpu.VMEM(seeds.shape, jnp.float32),
            pltpu.VMEM((RB + 1, *score), jnp.bfloat16),
            pltpu.SemaphoreType.DMA((8,)),
        ],
        name="first",
    )(*map(in_hbm, (seeds, deg_scale.reshape(RB, BLK), lists, col_index, row_offsets)))
    arranged = None
    for step in range(ITERS):
        chip = gather(gift, chips)
        opening = step == 0
        cross, inner = call(
            merge_kernel if opening else split_kernel,
            out_shape=(bf16(24 if opening else 16, *score), bf16(24, *score)),
            in_specs=[VMEM] * 2,
            out_specs=(VMEM,) * 2,
            scratch_shapes=[pltpu.VMEM((48, *score), jnp.bfloat16)] * opening,
            name="merge",
        )(mine, chip)
        sent, gathered = (pairs(1), pairs(0)) if opening else (all_pairs(2), all_pairs(1))
        cross = lax.ppermute(cross, "dom", sent + [(b, a) for a, b in sent])
        pair = gather(inner, gathered)
        if arranged is None:
            pair, row_offsets = lax.optimization_barrier((pair, row_offsets))
            arranged = call(
                arrange_kernel,
                out_shape=bf16(RB, 4 * BLK, BLK),
                in_specs=[HBM, HBM],
                out_specs=VMEM,
                scratch_shapes=[
                    pltpu.SMEM(row_offsets.shape, jnp.int32),
                    pltpu.VMEM(blocks.shape, jnp.bfloat16),
                    pltpu.SemaphoreType.DMA((9,)),
                ],
                cost_estimate=pl.CostEstimate(flops=0, bytes_accessed=16 << 20, transcendentals=0),
                name="arrange",
            )(in_hbm(row_offsets), in_hbm(blocks))
        owed = call(
            owe_kernel if opening else owe_later_kernel,
            out_shape=bf16(24, *score),
            in_specs=[VMEM] * 2,
            out_specs=VMEM,
            scratch_shapes=[pltpu.VMEM((48, *score), jnp.bfloat16)] * opening,
            name="owe",
        )(cross, pair)
        side = gather(owed, chips)
        last = step == ITERS - 1
        scratch = [pltpu.VMEM((ZERO + 1, *score), jnp.bfloat16)]
        if last:
            scratch += [pltpu.VMEM(seeds.shape, jnp.float32), pltpu.SemaphoreType.DMA((4,))]
        else:
            scratch += [
                pltpu.VMEM((RB + 1, *score), jnp.bfloat16),
                pltpu.SMEM(lists.shape, jnp.int32),
                pltpu.SemaphoreType.DMA,
            ]
        result = call(
            functools.partial(step_kernel, opening, last),
            out_shape=f32(*seeds.shape) if last else (bf16(RB, *score), bf16(32, *score), bf16(40, *score)),
            in_specs=[VMEM, ANY] + [VMEM] * 8,
            out_specs=HBM if last else (VMEM,) * 3,
            scratch_shapes=scratch,
            name="last" if last else "late",
        )(index, lists, x, chip, cross, pair, side, base, scale, arranged)
        if not last:
            x, mine, gift = result
    return result


def solution(mesh):
    in_specs = (
        P("dom", None, None),
        P("dom", None),
        P("dom", None),
        P("dom", None, None),
        P("dom"),
        P(None, "dom"),
    )
    out_specs = P(None, "dom")
    return jax.shard_map(
        functools.partial(on_device, mesh.size), mesh=mesh, in_specs=in_specs, out_specs=out_specs, check_vma=False
    )
```

```python
import functools

import jax
import jax.numpy as jnp
from jax import lax
from jax.experimental import pallas as pl
from jax.experimental.pallas import tpu as pltpu
from jax.sharding import PartitionSpec as P

ITERS = 4
ALPHA = 0.8
RB, C, BLK, HB = 32, 16, 128, 8
SENT, PAIR, SIDE, DIRECT, ZERO = 32, 56, 80, 104, 112


SMEM = pl.BlockSpec(memory_space=pltpu.SMEM)
VMEM = pl.BlockSpec(memory_space=pltpu.VMEM)
ANY = pl.BlockSpec(memory_space=pl.ANY)
HBM = pl.BlockSpec(memory_space=pltpu.HBM)


def in_hbm(value):
    return pltpu.with_memory_space_constraint(value, pltpu.HBM)


def bf16(*shape):
    return jax.ShapeDtypeStruct(shape, jnp.bfloat16)


def f32(*shape):
    return jax.ShapeDtypeStruct(shape, jnp.float32)


def role():
    me = lax.axis_index("dom")
    k = me & 1
    chip = me >> 1
    return k, ((chip ^ k) & 1) == 1, (((chip >> 1) ^ k) & 1) == 0


def units():
    k, up1, up2 = role()
    sel = jnp.where
    first = k == 0
    mine = [
        sel(first & ~up1, 1, -1),
        sel(up1, sel(first, 2, 0), -1),
        sel(first & up1, -1, sel(up1, 2, 3)),
        sel(up2, 4, 5),
    ]
    gift = [
        sel(first, sel(up1, 3, 2), sel(up1, -1, 2)),
        sel(first, sel(up1, 1, -1), sel(up1, 3, -1)),
        sel(first | up1, -1, 0),
        sel(up2, 5, 4),
        k,
    ]
    return mine, gift


def pack(lists, x, mine_out, gift_out):
    for out, which in zip((mine_out, gift_out), units()):
        for at, unit in enumerate(which):
            for h in range(HB):
                block = jnp.where(unit < 0, RB, lists[jnp.maximum(unit, 0), 0, h])
                out[at * HB + h] = x[block]


def places(columns, offsets):
    k, up1, up2 = role()
    sel = jnp.where
    first = k == 0
    near, far = sel(first, SENT, PAIR), sel(first, PAIR, SENT)
    base = [
        sel(first, sel(up1, SIDE + 8, near + 16), DIRECT),
        sel(first, DIRECT, sel(up1, near + 8, SIDE)),
        sel(up1, SIDE, sel(first, near + 8, near + 16)),
        sel(up1, near + 16, sel(first, SIDE, SIDE + 8)),
        sel(up2, SIDE + 16, far + 8),
        sel(up2, far + 8, SIDE + 16),
    ]
    where = columns
    for j in range(6):
        where = sel((columns - RB) >> 3 == j, base[j] + ((columns - RB) & (HB - 1)), where)
    where = jnp.broadcast_to((where - ZERO).astype(jnp.float32), (8, BLK)).astype(jnp.bfloat16)
    start, end = offsets[:, :RB], offsets[:, 1:]
    slots = lax.broadcasted_iota(jnp.int32, (BLK, RB), 0)
    rows = []
    for s in range(4):
        pick = sel((slots == start + s) & (slots < end), 1.0, 0.0).astype(jnp.bfloat16)
        rows.append(jnp.dot(where, pick, preferred_element_type=jnp.float32)[0:1].astype(jnp.int32) + ZERO)
    return rows


def first_kernel(*refs):
    sources, (x_out, mine_out, gift_out, base_out, scale_out) = refs[:3], refs[3:8]
    lists, seeds, x, sems = refs[8:]
    copies = []
    for i, target in enumerate((scale_out, lists)):
        copies.append(pltpu.make_async_copy(sources[i + 1], target, sems.at[i]))
    for i in range(4):
        part = pl.ds(i * RB * BLK // 4, RB * BLK // 4)
        copies.append(pltpu.make_async_copy(sources[0].at[:, part], seeds.at[:, part], sems.at[i + 2]))
    for copy in copies:
        copy.start()
    for copy in copies[:2]:
        copy.wait()
    for r in range(RB):
        if r % 8 == 0:
            copies[2 + r // 8].wait()
        field = seeds[:, r * BLK : (r + 1) * BLK]
        base_out[r] = (1.0 - ALPHA) * field
        x[r] = (field * scale_out[r : r + 1, :]).astype(jnp.bfloat16)
    x[RB] = jnp.zeros((C, BLK), jnp.bfloat16)
    x_out[...] = x[0:RB]
    pack(lists, x, mine_out, gift_out)


def partner(opening):
    me = lax.axis_index("dom")
    if opening:
        return 1 - jnp.where(me & 1 == 0, (me >> 2) & 1, (me >> 1) & 1)
    return ((me >> 1) ^ me) & 1


def merge_kernel(mine, chip, cross, inner, both):
    k = role()[0]
    sib = chip.at[1 - k]
    both[0:24] = mine[0:24] + sib[0:24]
    both[24:32] = sib[24:32]
    both[32:40] = mine[24:32]
    both[40:48] = mine[24:32]
    cross[...] = both[pl.ds(24 * k, 24)]
    inner[...] = both[pl.ds(24 - 24 * k, 24)]


def split_kernel(mine, chip, far, near):
    sib = chip.at[1 - role()[0]]
    near[...] = mine[0:24] + sib[0:24]
    far[0:8] = sib[24:32]
    far[8:16] = mine[24:32]


def owe_later_kernel(far, pair, out):
    out[0:16] = pair[partner(False), 0:16]
    out[16:24] = far[0:8]


def owe_kernel(cross, pair, out, both):
    k = role()[0]
    both[0:24] = cross[...]
    both[24:48] = pair[partner(True)]
    out[0:16] = both[pl.ds(24 * k, 16)]
    out[16:24] = both[pl.ds(24 - 24 * k, 8)]


def arrange_kernel(offsets_any, columns_hbm, blocks_hbm, out, index_out, offsets, starts, columns, blocks, sems):
    first = pltpu.make_async_copy(offsets_any, offsets, sems.at[8])
    first.start()
    tables = [
        pltpu.make_async_copy(offsets_any, starts, sems.at[9]),
        pltpu.make_async_copy(columns_hbm, columns, sems.at[10]),
    ]
    for table in tables:
        table.start()
    copies = []
    for g in range(8):
        part = pl.ds(16 * g, 16)
        copies.append(pltpu.make_async_copy(blocks_hbm.at[part], blocks.at[part], sems.at[g]))
        copies[-1].start()
    first.wait()
    for table in tables:
        table.wait()
    for s, row in enumerate(places(columns[...], starts[...])):
        index_out[s : s + 1, :] = row
    for g in range(8):
        copies[g].wait()
        for r in range(4 * g, 4 * g + 4):
            for s in range(4):
                slot = jnp.minimum(offsets[0, r] + s, 4 * r + 3)
                out[r, s * BLK : (s + 1) * BLK, :] = blocks[slot].T


def step_kernel(opening, last, index, lists_any, x_in, chip, cross, pair, side, base, scale, blocks, *rest):
    if last:
        out_hbm, src, out, sems = rest
        parts = []
        for i in range(4):
            part = pl.ds(i * 8 * BLK, 8 * BLK)
            parts.append(pltpu.make_async_copy(out.at[:, part], out_hbm.at[:, part], sems.at[i]))
    else:
        x_out, mine_out, gift_out, src, x, lists, sem = rest
        copy = pltpu.make_async_copy(lists_any, lists, sem)
        copy.start()
    k = role()[0]
    other = 1 - k
    src[0:SENT] = x_in[...]
    if opening:
        src[SENT:PAIR] = cross[...]
        src[PAIR:SIDE] = pair[partner(True)]
    else:
        src[pl.ds(SENT + 24 * k, 24)] = pair[partner(False)]
        src[pl.ds(PAIR - 24 * k, 16)] = cross[...]
    src[SIDE:DIRECT] = side[other]
    src[DIRECT:ZERO] = chip[other, 32:40]
    src[ZERO] = jnp.zeros((C, BLK), jnp.bfloat16)
    at = [index[s : s + 1, :] for s in range(4)]

    @pl.when(other >= 0)
    def _():
        for r in range(RB):
            lhs = jnp.concatenate([src[at[s][0, r]] for s in range(4)], axis=1)
            total = jnp.dot(lhs, blocks[r], preferred_element_type=jnp.float32)
            s = scale[r : r + 1, :]
            field = ALPHA * s * total + base[r]
            if last:
                out[:, r * BLK : (r + 1) * BLK] = field
                if r % 8 == 7:
                    parts[r // 8].start()
            else:
                x[r] = (field * s).astype(jnp.bfloat16)

    if last:
        for part in parts:
            part.wait()
    else:
        x[RB] = jnp.zeros((C, BLK), jnp.bfloat16)
        x_out[...] = x[0:RB]
        copy.wait()
        pack(lists, x, mine_out, gift_out)


def on_device(count, blocks, col_index, row_offsets, send_index, deg_scale, seeds):
    chips = [[2 * c, 2 * c + 1] for c in range(count // 2)]

    def pairs(crossing):
        found = []
        for c in range(len(chips)):
            if (c & 1) == crossing:
                found.append((2 * c + 1 - crossing, 2 * ((c + 1) % len(chips)) + 1 - crossing))
            if (c >> 1 & 1) == crossing:
                found.append((2 * c + crossing, 2 * ((c + 2) % len(chips)) + crossing))
        return found

    def all_pairs(step):
        found = []
        for c in range(len(chips)):
            core = (c >> 1) & 1 if step == 2 else 1 - (c & 1)
            found.append((2 * c + core, 2 * ((c + step) % len(chips)) + core))
        return found

    def gather(value, groups):
        return lax.all_gather(value, "dom", axis=0, axis_index_groups=[list(g) for g in groups], tiled=False)

    params = pltpu.CompilerParams(vmem_limit_bytes=16 << 20)
    call = functools.partial(pl.pallas_call, compiler_params=params)
    lists = jnp.transpose(send_index, (1, 0, 2))
    score = (C, BLK)

    x, mine, gift, base, scale = call(
        first_kernel,
        out_shape=(
            bf16(RB, *score),
            bf16(32, *score),
            bf16(40, *score),
            f32(RB, *score),
            f32(RB, BLK),
        ),
        in_specs=[HBM] * 3,
        out_specs=(VMEM,) * 5,
        scratch_shapes=[
            pltpu.SMEM(lists.shape, jnp.int32),
            pltpu.VMEM(seeds.shape, jnp.float32),
            pltpu.VMEM((RB + 1, *score), jnp.bfloat16),
            pltpu.SemaphoreType.DMA((6,)),
        ],
        name="first",
    )(*map(in_hbm, (seeds, deg_scale.reshape(RB, BLK), lists)))
    arranged = None
    for step in range(ITERS):
        chip = gather(gift, chips)
        opening = step == 0
        cross, inner = call(
            merge_kernel if opening else split_kernel,
            out_shape=(bf16(24 if opening else 16, *score), bf16(24, *score)),
            in_specs=[VMEM] * 2,
            out_specs=(VMEM,) * 2,
            scratch_shapes=[pltpu.VMEM((48, *score), jnp.bfloat16)] * opening,
            name="merge",
        )(mine, chip)
        sent, gathered = (pairs(1), pairs(0)) if opening else (all_pairs(2), all_pairs(1))
        cross = lax.ppermute(cross, "dom", sent + [(b, a) for a, b in sent])
        pair = gather(inner, gathered)
        if arranged is None:
            pair, row_offsets = lax.optimization_barrier((pair, row_offsets))
            arranged, index = call(
                arrange_kernel,
                out_shape=(bf16(RB, 4 * BLK, BLK), jax.ShapeDtypeStruct((4, RB), jnp.int32)),
                in_specs=[HBM] * 3,
                out_specs=(VMEM,) * 2,
                scratch_shapes=[
                    pltpu.SMEM(row_offsets.shape, jnp.int32),
                    pltpu.VMEM(row_offsets.shape, jnp.int32),
                    pltpu.VMEM(col_index.shape, jnp.int32),
                    pltpu.VMEM(blocks.shape, jnp.bfloat16),
                    pltpu.SemaphoreType.DMA((11,)),
                ],
                cost_estimate=pl.CostEstimate(flops=0, bytes_accessed=16 << 20, transcendentals=0),
                name="arrange",
            )(*map(in_hbm, (row_offsets, col_index, blocks)))
        owed = call(
            owe_kernel if opening else owe_later_kernel,
            out_shape=bf16(24, *score),
            in_specs=[VMEM] * 2,
            out_specs=VMEM,
            scratch_shapes=[pltpu.VMEM((48, *score), jnp.bfloat16)] * opening,
            name="owe",
        )(cross, pair)
        side = gather(owed, chips)
        last = step == ITERS - 1
        scratch = [pltpu.VMEM((ZERO + 1, *score), jnp.bfloat16)]
        if last:
            scratch += [pltpu.VMEM(seeds.shape, jnp.float32), pltpu.SemaphoreType.DMA((4,))]
        else:
            scratch += [
                pltpu.VMEM((RB + 1, *score), jnp.bfloat16),
                pltpu.SMEM(lists.shape, jnp.int32),
                pltpu.SemaphoreType.DMA,
            ]
        result = call(
            functools.partial(step_kernel, opening, last),
            out_shape=f32(*seeds.shape) if last else (bf16(RB, *score), bf16(32, *score), bf16(40, *score)),
            in_specs=[VMEM, ANY] + [VMEM] * 8,
            out_specs=HBM if last else (VMEM,) * 3,
            scratch_shapes=scratch,
            name="last" if last else "late",
        )(index, lists, x, chip, cross, pair, side, base, scale, arranged)
        if not last:
            x, mine, gift = result
    return result


def solution(mesh):
    in_specs = (
        P("dom", None, None),
        P("dom", None),
        P("dom", None),
        P("dom", None, None),
        P("dom"),
        P(None, "dom"),
    )
    out_specs = P(None, "dom")
    return jax.shard_map(
        functools.partial(on_device, mesh.size), mesh=mesh, in_specs=in_specs, out_specs=out_specs, check_vma=False
    )
```
